32 devices in a mesh: scene: 2 (over x), along: 16 (over z, y, core).
Axes of the slice: x: 2, y: 2, z: 4, core: 2. Of those that a mesh axis runs over, the one named last changes fastest.
Arguments:
- echoes: bfloat16 [2, 64, 16, 16, 256], P(None, ('scene', 'along')), parts along dimension 1, may hold values from -6 to 6
- integer_cell_displacement: int32 [64, 16], P(('scene', 'along')), parts along dimension 0, may hold values from 0 to 15
- fractional_level_label: int32 [64, 16], P(('scene', 'along')), parts along dimension 0, may hold values from 0 to 15
- steering: bfloat16 [2, 256, 256], replicated, may hold values from -0.25 to 0.25
- tile_anchor: int32 [32], P('scene'), parts along dimension 0, may hold values from -64 to 3904, as said below
Outputs:
- image_tiles: bfloat16 [2, 8192, 256], P(None, ('scene', 'along')), parts along dimension 1
The draws below stay inside these ranges and needn't reach their ends.
There are 2 independent parts, one for each index of `scene`. The reference program is written for one: setup_inputs(seed, part) draws one part's arguments, and reference() takes and returns one part's arrays. A program takes and returns all parts, laid end to end along the dimension named above; an argument that names none is the same for every part. Nothing has to cross between parts.
Inputs may be any that keep to these rules, and one draw needn't show every extreme that they name: tile_anchor[j] lies within 64 of j * 256.
All inputs are finite; a program needn't handle non-finite values.
Results may differ from the reference program's by a relative error of at most 0.0064.
Values may be sent and summed in bfloat16 or wider, within the bound.
A program may use at most 64 MiB of HBM per device.

```python
import math
import jax
import jax.numpy as jnp
from jax import lax

TX = 16
RX = 16
BEAMS = 256
BINS = 256
PULSE_DEV = 2
TILE_X = 256
STEPS = 16
TAPS = 8
SHIFTS = 16
FRACTION_LEVELS = 16
QUAD = 4093
WAVE_FOURTHS = 37
CHANS = 256
ECHO_TOTAL = 32
TILES = 16


def draw_tile_anchor(key, part):
    jitter = jax.random.randint(jax.random.fold_in(key, 7), (TILES,), -(TILE_X // 4), TILE_X // 4 + 1)
    return (jnp.arange(TILES, dtype=jnp.int32) * TILE_X + jitter).astype(jnp.int32)


def set_ends(array, rng, low, largest):
    longest = array.shape.index(max(array.shape))
    spots = []
    for shift in (0, 1):
        where = [jax.random.randint(jax.random.fold_in(rng, axis), (), 0, length) for axis, length in enumerate(array.shape)]
        where[longest] = (where[longest] + shift) % array.shape[longest]
        spots.append(tuple(where))
    return array.at[spots[0]].set(low).at[spots[1]].set(largest)


def block_scale(key, shape, shards, low, largest):
    def one(position, blocks):
        heights = jax.random.uniform(jax.random.fold_in(jax.random.fold_in(key, 6), position), (blocks,), jnp.float32, low / len(shards), largest / len(shards))
        return jnp.repeat(jnp.exp(heights), shape[position] // blocks).reshape((-1,) + (1,) * (len(shape) - position - 1))

    loudness = one(*shards[0])
    for cut in shards[1:]:
        loudness = loudness * one(*cut)
    return loudness


def noise(key, extent, spread, bound, split=(), kind=jnp.bfloat16):
    gain = block_scale(key, extent, split, -0.22, 0.18) if split else 1.0
    entries = jax.random.normal(key, extent, jnp.float32) * spread * gain
    return jnp.minimum(jnp.maximum(entries, -bound), bound).astype(kind)


def setup_inputs(seed: int = 0, part: int = 0) -> dict:
    seeds = jax.random.split(jax.random.key(seed), 6)
    own_keys = jax.random.split(jax.random.fold_in(seeds[5], part), 6)
    echoes = noise(own_keys[0], (2, ECHO_TOTAL, TX, RX, BINS), 1.0, 6.0, ((1, 16),))
    integer_cell_displacement = set_ends(jax.random.randint(own_keys[1], (ECHO_TOTAL, TX), 0, SHIFTS), jax.random.fold_in(own_keys[1], 1), 0, SHIFTS - 1).astype(jnp.int32)
    fractional_level_label = set_ends(jax.random.randint(own_keys[2], (ECHO_TOTAL, TX), 0, FRACTION_LEVELS), jax.random.fold_in(own_keys[2], 1), 0, FRACTION_LEVELS - 1).astype(jnp.int32)
    steering = noise(seeds[3], (2, CHANS, BEAMS), (2 * CHANS) ** -0.5, 0.25)
    tile_anchor = draw_tile_anchor(jax.random.fold_in(jax.random.fold_in(seeds[5], part), 71), part)
    return dict(echoes=echoes, integer_cell_displacement=integer_cell_displacement, fractional_level_label=fractional_level_label, steering=steering, tile_anchor=tile_anchor)


def tap_weights(integer_cell_displacement, fractional_level_label):
    fraction = fractional_level_label.astype(jnp.float32) / FRACTION_LEVELS
    tap_place = jnp.arange(TAPS, dtype=jnp.float32) - (TAPS // 2 - 1)
    displacement = tap_place[None, None, :] - fraction[..., None]
    window_taper = 0.54 + 0.46 * jnp.cos(math.pi * displacement / (TAPS // 2))
    kernel = jnp.sinc(displacement) * window_taper
    angle_turns = jnp.mod(WAVE_FOURTHS * (integer_cell_displacement * FRACTION_LEVELS + fractional_level_label), 4 * FRACTION_LEVELS).astype(jnp.float32) / (4 * FRACTION_LEVELS)
    phase_angle = 2.0 * math.pi * angle_turns
    return kernel * jnp.cos(phase_angle)[..., None], -kernel * jnp.sin(phase_angle)[..., None]


def compensate(echoes, integer_cell_displacement, fractional_level_label):
    bin_count = echoes.shape[-1]
    margin = SHIFTS // 2 + TAPS // 2
    padded = jnp.pad(echoes, ((0, 0), (0, 0), (0, 0), (0, 0), (margin, margin)))
    starts = (margin + integer_cell_displacement - SHIFTS // 2 - (TAPS // 2 - 1)).astype(jnp.int32)
    span_cells = bin_count + TAPS - 1

    def take_window(pulse_block, start):
        return lax.dynamic_slice_in_dim(pulse_block, start, span_cells, 2)

    windows = jax.vmap(jax.vmap(take_window, in_axes=(1, 0), out_axes=1), in_axes=(1, 0), out_axes=1)(padded, starts)
    coef_real, coef_imag = tap_weights(integer_cell_displacement, fractional_level_label)
    real_part = None
    imag_part = None
    for tap_index in range(TAPS):
        window_part = windows[..., tap_index:tap_index + bin_count]
        weight_real = coef_real[:, :, tap_index][:, :, None, None]
        weight_imag = coef_imag[:, :, tap_index][:, :, None, None]
        add_real = weight_real * window_part[0] - weight_imag * window_part[1]
        add_imag = weight_real * window_part[1] + weight_imag * window_part[0]
        real_part = add_real if real_part is None else real_part + add_real
        imag_part = add_imag if imag_part is None else imag_part + add_imag
    return jnp.stack([real_part, imag_part]).astype(jnp.bfloat16)


def form_beams(compensated, steering):
    pulse_count = compensated.shape[1]
    bin_count = compensated.shape[4]
    count_of_beams = steering.shape[2]
    flat_comp = compensated.reshape(2, pulse_count, -1, bin_count)
    mixer_grid = jnp.stack([jnp.concatenate([steering[0], steering[1]], 1),
                            jnp.concatenate([-steering[1], steering[0]], 1)])
    formed = jnp.einsum("pkcw,pcq->qkw", flat_comp.astype(jnp.float32), mixer_grid.astype(jnp.float32))
    return formed.reshape(2, count_of_beams, pulse_count, bin_count).astype(jnp.bfloat16)


def phase_table(count_of_beams, pulse_count, source, anchor):
    pulse_numbers = jnp.arange(pulse_count, dtype=jnp.int32)
    pixels = jnp.arange(TILE_X, dtype=jnp.int32)
    pixel_ratio = TILE_X // pulse_count
    pulse_spot = (source * pulse_count + pulse_numbers) * pixel_ratio
    offset_cells = anchor + pixels[None, :] - pulse_spot[:, None]
    beam_ids = jnp.arange(count_of_beams, dtype=jnp.int32)
    displacement_residue = jnp.mod(offset_cells, QUAD).astype(jnp.int32)
    offset_square = jnp.mod(displacement_residue * displacement_residue, QUAD).astype(jnp.int32)
    beam_square = jnp.mod(beam_ids * beam_ids, QUAD).astype(jnp.int32)
    phase_units = jnp.mod(offset_square[None] + beam_square[:, None, None] * displacement_residue[None]
                          + beam_ids[:, None, None] * offset_square[None], QUAD).astype(jnp.int32)
    phase_angle = 2.0 * math.pi * (phase_units.astype(jnp.float32) / QUAD)
    gain_norm = (STEPS * pulse_count * count_of_beams) ** -0.5
    grid_real = (gain_norm * jnp.cos(phase_angle)).astype(jnp.bfloat16)
    grid_imag = (gain_norm * jnp.sin(phase_angle)).astype(jnp.bfloat16)
    return jnp.stack([jnp.concatenate([grid_real, grid_imag], -1),
                      jnp.concatenate([-grid_imag, grid_real], -1)])


def project(beam_data, source, anchor):
    phase_grid = phase_table(beam_data.shape[1], beam_data.shape[2], source, anchor)
    summed = jnp.einsum("pakq,pakw->qw", phase_grid.astype(jnp.float32), beam_data.astype(jnp.float32))
    return summed.reshape(2, TILE_X, beam_data.shape[3])


def reference(echoes, integer_cell_displacement, fractional_level_label, steering, tile_anchor):
    beam_data = form_beams(compensate(echoes, integer_cell_displacement, fractional_level_label), steering)

    def one_tile(tile_id):
        running = jnp.zeros((2, TILE_X, BINS), jnp.float32)
        for distance in range(STEPS):
            source = tile_id - distance
            inside = source >= 0
            clamped = jnp.maximum(source, 0).astype(jnp.int32)
            pulse_block = lax.dynamic_slice_in_dim(beam_data, clamped * PULSE_DEV, PULSE_DEV, 2)
            contrib = project(pulse_block, clamped, tile_anchor[tile_id])
            running = running + jnp.where(inside, contrib, jnp.zeros_like(contrib))
        return running

    tile_sums = lax.map(one_tile, jnp.arange(TILES, dtype=jnp.int32))
    image_tiles = tile_sums.transpose(1, 0, 2, 3).reshape(2, TILES * TILE_X, BINS)
    return image_tiles.astype(jnp.bfloat16)
```

```python
import functools

import jax
import jax.numpy as jnp
import numpy as np
from jax import lax
from jax.experimental import pallas as pl
from jax.experimental.pallas import tpu as pltpu
from jax.sharding import PartitionSpec as P

TILE_X = 256
STEPS = 16
TAPS = 8
SHIFTS = 16
FRACTION_LEVELS = 16
QUAD = 4093
WAVE_FOURTHS = 37
LANES = 128
SLAB = 16
JITTER = TILE_X // 4
GROUP = 4
CORES = 2
PAIR = GROUP // CORES
REACH = STEPS // GROUP
HALVES = 2
CHUNKS = 2
CYCLE = 4 * FRACTION_LEVELS
MESH = pl.DeviceIdType.MESH


def scalar_table():
    shift = np.arange(TAPS)[None] - (TAPS // 2 - 1) - np.arange(FRACTION_LEVELS)[:, None] / FRACTION_LEVELS
    kernel = np.sinc(shift) * (0.54 + 0.46 * np.cos(np.pi * shift / (TAPS // 2)))
    theta = 2 * np.pi * np.arange(CYCLE) / CYCLE
    return np.concatenate([kernel.ravel(), np.cos(theta), np.sin(theta)]).astype(np.float32)


def phase_table(beams, pulses, first, rows):
    offset = np.mod(np.arange(first, first + rows, dtype=np.int64), QUAD)[:, None]
    beam = np.arange(beams, dtype=np.int64)[None]
    units = (offset * offset + beam * beam * offset + beam * offset * offset) % QUAD
    phi = 2 * np.pi * units / QUAD
    gain = (STEPS * pulses * beams) ** -0.5
    table = gain * np.concatenate([np.cos(phi), np.sin(phi)], 1)
    return table.reshape(rows // SLAB, SLAB, 2 * beams).astype(jnp.bfloat16)


def compensate(pulse, cells, levels, scalars, echoes, straight):
    _, _, transmitters, receivers, bins = echoes.shape
    columns = bins // LANES
    lane = lax.broadcasted_iota(jnp.int32, (2 * receivers, LANES), 1)

    @pl.loop(0, transmitters, unroll=4)
    def _(sender):
        cell, level = cells[pulse, sender], levels[pulse, sender]
        units = lax.rem(WAVE_FOURTHS * (cell * FRACTION_LEVELS + level), CYCLE)
        cosine = scalars[FRACTION_LEVELS * TAPS + units]
        sine = scalars[FRACTION_LEVELS * TAPS + CYCLE + units]
        both = jnp.concatenate([echoes[0, pulse, sender], echoes[1, pulse, sender]], 0)
        both = both.astype(jnp.float32)
        back = SHIFTS - cell
        turned = [
            pltpu.roll(both[:, c * LANES : (c + 1) * LANES], back, 1) for c in range(columns)
        ]
        keep = lane >= back
        zero = jnp.zeros_like(turned[0])
        base = [
            jnp.where(keep, turned[c] if c < columns else zero, turned[c - 1] if c else zero)
            for c in range(columns + 1)
        ]
        sums = [None] * columns
        for tap in range(TAPS):
            ahead = tap + SHIFTS // 2 - (TAPS // 2 - 1)
            weight = scalars[level * TAPS + tap]
            moved = [pltpu.roll(b, LANES - ahead, 1) for b in base]
            for c in range(columns):
                piece = weight * jnp.where(lane < LANES - ahead, moved[c], moved[c + 1])
                sums[c] = piece if tap == 0 else sums[c] + piece
        rows = pl.ds(pl.multiple_of(sender * receivers, receivers), receivers)
        for half in range(HALVES):
            a, b = sums[half][:receivers], sums[half][receivers:]
            straight[half, rows, :LANES] = (cosine * a + sine * b).astype(jnp.bfloat16)
            straight[half, rows, LANES:] = (cosine * b - sine * a).astype(jnp.bfloat16)


def image_kernel(
    count, far_anchors, far_cells, far_levels, far_scalars, far_echoes, far_steering, far_table, image,
    anchors, cells, levels, scalars, echoes, steering, table, fetched,
    straight, turned, outbox, got, total, held, own, final, outgoing, incoming, arrived, across_out, across_in,
    mate_send, mate_recv, side_send, side_recv, pass_send, pass_recv,
    up_send, up_recv, last_send, last_recv, across_send, across_recv,
):
    pulses = echoes.shape[1]
    beams = steering.shape[2]
    spacing = TILE_X // pulses
    window = TILE_X + SLAB
    quarter = LANES // CHUNKS
    pieces = [
        (far_cells, cells), (far_levels, levels), (far_scalars, scalars),
        *[(far_echoes.at[:, pulse], echoes.at[:, pulse]) for pulse in range(pulses)],
        (far_steering, steering), (far_anchors, anchors), (far_table, table),
    ]
    fetches = [
        pltpu.make_async_copy(source, landing, fetched.at[number])
        for number, (source, landing) in enumerate(pieces)
    ]
    for fetch in fetches:
        fetch.start()
    small, fetch_echoes = fetches[:3], fetches[3 : 3 + pulses]
    fetch_steering, fetch_anchors, fetch_table = fetches[3 + pulses :]
    me = lax.axis_index("along")
    group, place = me // GROUP, me % GROUP
    chip, core = place // CORES, place % CORES
    groups = count // GROUP
    mate_place, side_place = chip * CORES + 1 - core, (1 - chip) * CORES + core
    far_place = GROUP - 1 - place
    mate, side = group * GROUP + mate_place, group * GROUP + side_place
    has_below, has_above = group > 0, group < groups - 1

    barrier = pltpu.get_barrier_semaphore()

    def greet(other):
        pl.semaphore_signal(barrier, inc=1, device_id={"along": other}, device_id_type=MESH)

    greet(mate)
    greet(side)

    @pl.when(has_below)
    def _():
        greet(me - GROUP)
        greet(side - GROUP)

    @pl.when(has_above)
    def _():
        greet(me + GROUP)
        greet(side + GROUP)

    def remote(source, landing, send, recv, device):
        return pltpu.make_async_remote_copy(
            src_ref=source, dst_ref=landing, send_sem=send, recv_sem=recv,
            device_id={"along": device}, device_id_type=MESH,
        )

    def to_side(chunk, pulse):
        return remote(
            outbox.at[chunk, pulse], got.at[chunk, place, pulse],
            side_send.at[chunk, pulse], side_recv.at[chunk, pulse], side,
        )

    def to_mate(chunk, pulse):
        mine = got.at[chunk, place, pulse]
        return remote(mine, mine, mate_send.at[chunk, pulse], mate_recv.at[chunk, pulse], mate)

    def pass_on(chunk, pulse):
        theirs = got.at[chunk, side_place, pulse]
        return remote(theirs, theirs, pass_send.at[chunk, pulse], pass_recv.at[chunk, pulse], mate)

    def to_above(step, pick, chunk):
        return remote(
            outgoing.at[step - 1, pick, chunk], incoming.at[step - 2, pick, chunk],
            up_send.at[step - 2, pick, chunk], up_recv.at[step - 2, pick, chunk], me + GROUP,
        )

    def to_owner(pick, chunk):
        return remote(
            outgoing.at[0, pick, chunk], arrived.at[chip, chunk],
            last_send.at[pick, chunk], last_recv.at[chip, chunk],
            (group + 1) * GROUP + core + CORES * pick,
        )

    def from_below(half, chunk):
        return remote(
            arrived.at[half, chunk], arrived.at[half, chunk],
            last_send.at[half, chunk], last_recv.at[half, chunk], side,
        )

    def across(chunk):
        return remote(
            across_out.at[chunk], across_in.at[chunk], across_send.at[chunk], across_recv.at[chunk], side
        )

    first_lanes = lax.broadcasted_iota(jnp.int32, (beams, LANES), 1) < quarter

    def form(pulse, half):
        one = jnp.dot(turned[0], straight[half], preferred_element_type=jnp.float32)
        two = jnp.dot(turned[1], straight[half], preferred_element_type=jnp.float32)
        real, imag = one[:, :LANES] - two[:, LANES:], one[:, LANES:] + two[:, :LANES]
        return (
            jnp.where(first_lanes, real, pltpu.roll(imag, quarter, 1)).astype(jnp.bfloat16),
            jnp.where(first_lanes, pltpu.roll(real, quarter, 1), imag).astype(jnp.bfloat16),
        )

    for pulse in range(pulses):
        if pulse == 0:
            for fetch in small:
                fetch.wait()
        fetch_echoes[pulse].wait()
        compensate(pulse, cells, levels, scalars, echoes, straight)
        if pulse == 0:
            fetch_steering.wait()
            turned[0] = steering[0].T
            turned[1] = steering[1].T
        for chunk, block in enumerate(form(pulse, 1 - chip)):
            outbox[chunk, pulse] = block
        if pulse == 0:
            pl.semaphore_wait(
                barrier, 2 + 2 * has_below.astype(jnp.int32) + 2 * has_above.astype(jnp.int32)
            )
        to_side(0, pulse).start()
        for chunk, block in enumerate(form(pulse, chip)):
            got[chunk, place, pulse] = block
        to_mate(0, pulse).start()
    for chunk in range(1, CHUNKS):
        for pulse in range(pulses):
            to_side(chunk, pulse).start()
            to_mate(chunk, pulse).start()

    def reaches(step):
        return group + step < groups

    def forward(chunk):
        for pulse in range(pulses):
            to_side(chunk, pulse).wait_recv()
            pass_on(chunk, pulse).start()

    def collect(chunk):
        for pulse in range(pulses):
            to_mate(chunk, pulse).wait_recv()
            pass_on(chunk, pulse).wait_recv()

    row = lax.broadcasted_iota(jnp.int32, (TILE_X // 8, 8, LANES), 1)
    low_lanes = lax.broadcasted_iota(jnp.int32, (window, LANES), 1) < quarter

    def jitter(step, pick):
        tile = (group + step) * GROUP + core + CORES * pick
        return jnp.clip(anchors[tile] - tile * TILE_X, -JITTER, JITTER) + JITTER

    def term(step, pick, chunk, source, pulse, aligned):
        blocks = GROUP * step + core + CORES * pick - source
        start = TILE_X // SLAB * blocks + spacing // SLAB * (pulses - 1 - pulse)
        slabs = pl.ds(start + aligned, window // SLAB)
        turns = [table[slabs, :, cut].reshape(window, beams) for cut in (slice(0, beams), slice(beams, 2 * beams))]
        turns = jnp.concatenate(turns, 0)
        return jnp.dot(turns, got[chunk, source, pulse], preferred_element_type=jnp.float32)

    def combine_parts(both):
        second = pltpu.roll(both[window:], quarter, 1)
        return both[:window] + jnp.where(low_lanes, -second, second)

    def settle(value, offset):
        late = jnp.full((window - 8, LANES), offset, jnp.int32) >= 8
        value = jnp.where(late, value[8:], value[:-8])
        value = value.reshape(TILE_X // 8 + 1, 8, LANES)
        ahead = lax.rem(offset, 8)
        value = pltpu.roll(value, lax.rem(8 - ahead, 8), 1)
        value = jnp.where(row < 8 - ahead, value[:-1], value[1:])
        return value.reshape(TILE_X, LANES)

    def project(step, pick, chunk, low, high):
        shift = jitter(step, pick)
        aligned, offset = lax.div(shift, SLAB), lax.rem(shift, SLAB)
        if low is None:
            both = None
            for source in range(GROUP):
                for pulse in range(pulses):
                    add = term(step, pick, chunk, source, pulse, aligned)
                    both = add if both is None else both + add
            return settle(combine_parts(both), offset)
        total[...] = jnp.zeros(total.shape, jnp.float32)

        @pl.loop(low, high)
        def _(source):
            both = None
            for pulse in range(pulses):
                add = term(step, pick, chunk, source, pulse, aligned)
                both = add if both is None else both + add
            total[...] += combine_parts(both)

        return settle(total[...], offset)

    def send(step, pick, chunk, value):
        outgoing[step - 1, pick, chunk] = value.astype(jnp.bfloat16)
        pl.when(step > 1)(lambda: to_above(step, pick, chunk).start())
        pl.when(step == 1)(lambda: to_owner(pick, chunk).start())

    def begin(chunk):
        @pl.when(reaches(REACH))
        def _():
            for pick in range(PAIR):
                send(REACH, pick, chunk, project(REACH, pick, chunk, core + CORES * pick + 1, GROUP))

        @pl.loop(0, (REACH - 1) * PAIR)
        def _(item):
            step, pick = REACH - 1 - item // PAIR, item % PAIR

            @pl.when(reaches(step))
            def _():
                value = project(step, pick, chunk, None, None)

                @pl.when(has_below)
                def _():
                    held[step - 1, pick, chunk] = value

                @pl.when(jnp.logical_not(has_below))
                def _():
                    send(step, pick, chunk, value)

    def combine(chunk):
        @pl.loop(0, (REACH - 1) * PAIR)
        def _(item):
            step, pick = REACH - 1 - item // PAIR, item % PAIR

            @pl.when(has_below & reaches(step))
            def _():
                to_above(step + 1, pick, chunk).wait_recv()
                value = held[step - 1, pick, chunk] + incoming[step - 1, pick, chunk].astype(jnp.float32)
                send(step, pick, chunk, value)

    def own_group(chunk):
        value = project(0, 1 - chip, chunk, 0, core + CORES * (1 - chip) + 1)
        across_out[chunk] = value.astype(jnp.bfloat16)
        across(chunk).start()
        own[chunk] = project(0, chip, chunk, 0, place + 1)

    final_lanes = lax.broadcasted_iota(jnp.int32, (TILE_X, LANES), 1) < quarter

    def finish():
        for chunk in range(CHUNKS):
            across(chunk).wait_recv()
        for half in range(HALVES):
            for chunk in range(CHUNKS):
                mine, theirs = own[chunk], across_in[chunk].astype(jnp.float32)
                final[half, chunk] = jnp.where(chip == half, mine, theirs)

        @pl.when(has_below)
        def _():
            for chunk in range(CHUNKS):
                for half in range(HALVES):
                    from_below(half, chunk).wait_recv()
                    final[half, chunk] += arrived[half, chunk].astype(jnp.float32)

        for half in range(HALVES):
            one, two = final[half, 0], final[half, 1]
            cut = slice(half * LANES, (half + 1) * LANES)
            real = jnp.where(final_lanes, one, pltpu.roll(two, quarter, 1))
            imag = jnp.where(final_lanes, pltpu.roll(one, quarter, 1), two)
            image[0, :, cut] = real.astype(jnp.bfloat16)
            image[1, :, cut] = imag.astype(jnp.bfloat16)

    forward(0)
    fetch_anchors.wait()
    fetch_table.wait()
    collect(0)
    begin(0)
    combine(0)
    for chunk in range(1, CHUNKS):
        forward(chunk)
        collect(chunk)
        begin(chunk)
    for chunk in range(CHUNKS):
        own_group(chunk)
    for chunk in range(1, CHUNKS):
        combine(chunk)
    finish()

    for chunk in range(CHUNKS):
        for pulse in range(pulses):
            to_side(chunk, pulse).wait_send()
            to_mate(chunk, pulse).wait_send()
            pass_on(chunk, pulse).wait_send()
        across(chunk).wait_send()
        for pick in range(PAIR):
            for step in range(2, REACH + 1):
                pl.when(reaches(step))(to_above(step, pick, chunk).wait_send)
            pl.when(has_above)(to_owner(pick, chunk).wait_send)


def local(count, echoes, integer_cell_displacement, fractional_level_label, steering, tile_anchor):
    pulses, bins = echoes.shape[1], echoes.shape[4]
    channels, beams = steering.shape[1:]
    spacing = TILE_X // pulses
    first = -JITTER - spacing * (pulses - 1)
    rows = TILE_X * (STEPS - 1) + spacing * (pulses - 1) + 2 * JITTER + TILE_X + SLAB
    table = jnp.asarray(phase_table(beams, pulses, first, rows))
    scalars = jnp.asarray(scalar_table())
    pair = (CHUNKS, pulses)
    dma = pltpu.SemaphoreType.DMA
    narrow = (TILE_X, LANES)
    return pl.pallas_call(
        functools.partial(image_kernel, count),
        out_shape=jax.ShapeDtypeStruct((2, TILE_X, bins), jnp.bfloat16),
        in_specs=[pl.BlockSpec(memory_space=pltpu.HBM)] * 7,
        out_specs=pl.BlockSpec(memory_space=pltpu.VMEM),
        scratch_shapes=[
            pltpu.SMEM(tile_anchor.shape, jnp.int32),
            pltpu.SMEM(integer_cell_displacement.shape, jnp.int32),
            pltpu.SMEM(fractional_level_label.shape, jnp.int32),
            pltpu.SMEM(scalars.shape, jnp.float32),
            pltpu.VMEM(echoes.shape, echoes.dtype),
            pltpu.VMEM(steering.shape, steering.dtype),
            pltpu.VMEM(table.shape, table.dtype),
            dma((6 + pulses,)),
            pltpu.VMEM((HALVES, channels, 2 * LANES), jnp.bfloat16),
            pltpu.VMEM((2, beams, channels), jnp.bfloat16),
            pltpu.VMEM((CHUNKS, pulses, beams, LANES), jnp.bfloat16),
            pltpu.VMEM((CHUNKS, GROUP, pulses, beams, LANES), jnp.bfloat16),
            pltpu.VMEM((TILE_X + SLAB, LANES), jnp.float32),
            pltpu.VMEM((REACH - 1, PAIR, CHUNKS, *narrow), jnp.float32),
            pltpu.VMEM((CHUNKS, *narrow), jnp.float32),
            pltpu.VMEM((HALVES, CHUNKS, *narrow), jnp.float32),
            pltpu.VMEM((REACH, PAIR, CHUNKS, *narrow), jnp.bfloat16),
            pltpu.VMEM((REACH - 1, PAIR, CHUNKS, *narrow), jnp.bfloat16),
            pltpu.VMEM((HALVES, CHUNKS, *narrow), jnp.bfloat16),
            pltpu.VMEM((CHUNKS, *narrow), jnp.bfloat16),
            pltpu.VMEM((CHUNKS, *narrow), jnp.bfloat16),
            dma(pair), dma(pair), dma(pair), dma(pair), dma(pair), dma(pair),
            dma((REACH - 1, PAIR, CHUNKS)), dma((REACH - 1, PAIR, CHUNKS)),
            dma((PAIR, CHUNKS)), dma((HALVES, CHUNKS)), dma((CHUNKS,)), dma((CHUNKS,)),
        ],
        compiler_params=pltpu.CompilerParams(
            collective_id=0, has_side_effects=True, vmem_limit_bytes=67_043_328
        ),
        name="image",
    )(tile_anchor, integer_cell_displacement, fractional_level_label, scalars, echoes, steering, table)


def solution(mesh):
    placed = (
        P(None, ("scene", "along"), None, None, None),
        P(("scene", "along"), None),
        P(("scene", "along"), None),
        P(),
        P("scene"),
    )
    return jax.shard_map(
        functools.partial(local, mesh.shape["along"]),
        mesh=mesh,
        in_specs=placed,
        out_specs=P(None, ("scene", "along"), None),
        check_vma=False,
    )
```

```python
import functools

import jax
import jax.numpy as jnp
import numpy as np
from jax import lax
from jax.experimental import pallas as pl
from jax.experimental.pallas import tpu as pltpu
from jax.sharding import PartitionSpec as P

TILE_X = 256
STEPS = 16
TAPS = 8
SHIFTS = 16
FRACTION_LEVELS = 16
QUAD = 4093
WAVE_FOURTHS = 37
LANES = 128
SLAB = 16
JITTER = TILE_X // 4
GROUP = 4
CORES = 2
PAIR = GROUP // CORES
REACH = STEPS // GROUP
HALVES = 2
CHUNKS = 2
CYCLE = 4 * FRACTION_LEVELS
MESH = pl.DeviceIdType.MESH


def scalar_table():
    shift = np.arange(TAPS)[None] - (TAPS // 2 - 1) - np.arange(FRACTION_LEVELS)[:, None] / FRACTION_LEVELS
    kernel = np.sinc(shift) * (0.54 + 0.46 * np.cos(np.pi * shift / (TAPS // 2)))
    theta = 2 * np.pi * np.arange(CYCLE) / CYCLE
    return np.concatenate([kernel.ravel(), np.cos(theta), np.sin(theta)]).astype(np.float32)


def phase_table(beams, pulses, first, rows):
    offset = np.mod(np.arange(first, first + rows, dtype=np.int64), QUAD)[:, None]
    beam = np.arange(beams, dtype=np.int64)[None]
    units = (offset * offset + beam * beam * offset + beam * offset * offset) % QUAD
    phi = 2 * np.pi * units / QUAD
    gain = (STEPS * pulses * beams) ** -0.5
    table = gain * np.concatenate([np.cos(phi), np.sin(phi)], 1)
    return table.reshape(rows // SLAB, SLAB, 2 * beams).astype(jnp.bfloat16)


def compensate(pulse, cells, levels, scalars, echoes, straight):
    _, _, transmitters, receivers, bins = echoes.shape
    columns = bins // LANES
    lane = lax.broadcasted_iota(jnp.int32, (2 * receivers, LANES), 1)
    reach_back = SHIFTS // 2 + TAPS // 2 - 1

    def ahead(parts, count):
        moved = [pltpu.roll(part, LANES - count, 1) for part in parts]
        inside = lane < LANES - count
        return [jnp.where(inside, a, b) for a, b in zip(moved[:-1], moved[1:])] + moved[-1:]

    @pl.loop(0, transmitters, unroll=4)
    def _(sender):
        cell, level = cells[pulse, sender], levels[pulse, sender]
        units = lax.rem(WAVE_FOURTHS * (cell * FRACTION_LEVELS + level), CYCLE)
        cosine = scalars[FRACTION_LEVELS * TAPS + units]
        sine = scalars[FRACTION_LEVELS * TAPS + CYCLE + units]
        both = jnp.concatenate([echoes[0, pulse, sender], echoes[1, pulse, sender]], 0)
        both = both.astype(jnp.float32)
        back = reach_back - cell
        zero = jnp.zeros(lane.shape, jnp.float32)
        turned = [
            pltpu.roll(both[:, c * LANES : (c + 1) * LANES], lax.rem(LANES + back, LANES), 1)
            for c in range(columns)
        ]
        turned = [zero, *turned, zero, zero]
        low, high = lane < back, lane >= LANES + back
        base = [
            jnp.where(low, turned[c], jnp.where(high, turned[c + 2], turned[c + 1]))
            for c in range(columns + 1)
        ]
        near, far = [None] * (columns + 1), [None] * (columns + 1)
        for tap in range(TAPS // 2):
            shifted = ahead(base, tap) if tap else base
            weight = scalars[level * TAPS + tap]
            later = scalars[level * TAPS + TAPS // 2 + tap]
            for c in range(columns + 1):
                near[c] = weight * shifted[c] + (near[c] if tap else 0.0)
                far[c] = later * shifted[c] + (far[c] if tap else 0.0)
        sums = [a + b for a, b in zip(near[:columns], ahead(far, TAPS // 2))]
        rows = pl.ds(pl.multiple_of(sender * receivers, receivers), receivers)
        for half in range(HALVES):
            a, b = sums[half][:receivers], sums[half][receivers:]
            straight[half, rows, :LANES] = (cosine * a + sine * b).astype(jnp.bfloat16)
            straight[half, rows, LANES:] = (cosine * b - sine * a).astype(jnp.bfloat16)


def image_kernel(
    count, far_anchors, far_cells, far_levels, far_scalars, far_echoes, far_steering, far_table, image,
    anchors, cells, levels, scalars, echoes, steering, table, fetched,
    straight, turned, outbox, got, held, own, final, outgoing, incoming, arrived, across_out, across_in,
    mate_send, mate_recv, side_send, side_recv, pass_send, pass_recv,
    up_send, up_recv, last_send, last_recv, across_send, across_recv,
):
    pulses = echoes.shape[1]
    beams = steering.shape[2]
    spacing = TILE_X // pulses
    window = TILE_X + SLAB
    quarter = LANES // CHUNKS
    pieces = [
        (far_cells, cells), (far_levels, levels), (far_scalars, scalars),
        *[(far_echoes.at[:, pulse], echoes.at[:, pulse]) for pulse in range(pulses)],
        (far_steering, steering), (far_anchors, anchors), (far_table, table),
    ]
    fetches = [
        pltpu.make_async_copy(source, landing, fetched.at[number])
        for number, (source, landing) in enumerate(pieces)
    ]
    for fetch in fetches:
        fetch.start()
    small, fetch_echoes = fetches[:3], fetches[3 : 3 + pulses]
    fetch_steering, fetch_anchors, fetch_table = fetches[3 + pulses :]
    me = lax.axis_index("along")
    group, place = me // GROUP, me % GROUP
    chip, core = place // CORES, place % CORES
    groups = count // GROUP
    mate_place, side_place = chip * CORES + 1 - core, (1 - chip) * CORES + core
    far_place = GROUP - 1 - place
    mate, side = group * GROUP + mate_place, group * GROUP + side_place
    has_below, has_above = group > 0, group < groups - 1

    barrier = pltpu.get_barrier_semaphore()

    def greet(other):
        pl.semaphore_signal(barrier, inc=1, device_id={"along": other}, device_id_type=MESH)

    greet(mate)
    greet(side)

    @pl.when(has_below)
    def _():
        greet(me - GROUP)
        greet(side - GROUP)

    @pl.when(has_above)
    def _():
        greet(me + GROUP)
        greet(side + GROUP)

    def remote(source, landing, send, recv, device):
        return pltpu.make_async_remote_copy(
            src_ref=source, dst_ref=landing, send_sem=send, recv_sem=recv,
            device_id={"along": device}, device_id_type=MESH,
        )

    def to_side(chunk, pulse):
        return remote(
            outbox.at[chunk, pulse], got.at[chunk, place, pulse],
            side_send.at[chunk, pulse], side_recv.at[chunk, pulse], side,
        )

    def to_mate(chunk, pulse):
        mine = got.at[chunk, place, pulse]
        return remote(mine, mine, mate_send.at[chunk, pulse], mate_recv.at[chunk, pulse], mate)

    def pass_on(chunk, pulse):
        theirs = got.at[chunk, side_place, pulse]
        return remote(theirs, theirs, pass_send.at[chunk, pulse], pass_recv.at[chunk, pulse], mate)

    def to_above(step, pick, chunk):
        return remote(
            outgoing.at[step - 1, pick, chunk], incoming.at[step - 2, pick, chunk],
            up_send.at[step - 2, pick, chunk], up_recv.at[step - 2, pick, chunk], me + GROUP,
        )

    def to_owner(pick, chunk):
        return remote(
            outgoing.at[0, pick, chunk], arrived.at[chip, chunk],
            last_send.at[pick, chunk], last_recv.at[chip, chunk],
            (group + 1) * GROUP + core + CORES * pick,
        )

    def from_below(half, chunk):
        return remote(
            arrived.at[half, chunk], arrived.at[half, chunk],
            last_send.at[half, chunk], last_recv.at[half, chunk], side,
        )

    def across(chunk):
        return remote(
            across_out.at[chunk], across_in.at[chunk], across_send.at[chunk], across_recv.at[chunk], side
        )

    every = tuple(range(CHUNKS))
    first_lanes = lax.broadcasted_iota(jnp.int32, (beams, LANES), 1) < quarter

    def form(pulse, half):
        one = jnp.dot(turned[0], straight[half], preferred_element_type=jnp.float32)
        two = jnp.dot(turned[1], straight[half], preferred_element_type=jnp.float32)
        real, imag = one[:, :LANES] - two[:, LANES:], one[:, LANES:] + two[:, :LANES]
        return (
            jnp.where(first_lanes, real, pltpu.roll(imag, quarter, 1)).astype(jnp.bfloat16),
            jnp.where(first_lanes, pltpu.roll(real, quarter, 1), imag).astype(jnp.bfloat16),
        )

    for pulse in range(pulses):
        if pulse == 0:
            for fetch in small:
                fetch.wait()
        fetch_echoes[pulse].wait()
        compensate(pulse, cells, levels, scalars, echoes, straight)
        if pulse == 0:
            fetch_steering.wait()
            turned[0] = steering[0].T
            turned[1] = steering[1].T
        for chunk, block in enumerate(form(pulse, 1 - chip)):
            outbox[chunk, pulse] = block
        if pulse == 0:
            pl.semaphore_wait(
                barrier, 2 + 2 * has_below.astype(jnp.int32) + 2 * has_above.astype(jnp.int32)
            )
        to_side(0, pulse).start()
        for chunk, block in enumerate(form(pulse, chip)):
            got[chunk, place, pulse] = block
        to_mate(0, pulse).start()
    for chunk in range(1, CHUNKS):
        for pulse in range(pulses):
            to_side(chunk, pulse).start()
            to_mate(chunk, pulse).start()

    def reaches(step):
        return group + step < groups

    def forward(chunk):
        for pulse in range(pulses):
            to_side(chunk, pulse).wait_recv()
            pass_on(chunk, pulse).start()

    def collect(chunk):
        for pulse in range(pulses):
            to_mate(chunk, pulse).wait_recv()
            pass_on(chunk, pulse).wait_recv()

    row = lax.broadcasted_iota(jnp.int32, (TILE_X // 8, 8, LANES), 1)
    low_lanes = lax.broadcasted_iota(jnp.int32, (window, LANES), 1) < quarter

    def jitter(step, pick):
        tile = (group + step) * GROUP + core + CORES * pick
        return jnp.clip(anchors[tile] - tile * TILE_X, -JITTER, JITTER) + JITTER

    def term(step, pick, chunks, source, pulse, aligned, guard):
        blocks = GROUP * step + core + CORES * pick - source
        if guard is not None:
            blocks = jnp.clip(blocks, 0, STEPS - 1)
        start = TILE_X // SLAB * blocks + spacing // SLAB * (pulses - 1 - pulse)
        slabs = pl.ds(start + aligned, window // SLAB)
        turns = [table[slabs, :, cut].reshape(window, beams) for cut in (slice(0, beams), slice(beams, 2 * beams))]
        turns = jnp.concatenate(turns, 0)
        parts = [got[chunk, source, pulse] for chunk in chunks]
        parts = parts[0] if len(parts) == 1 else jnp.concatenate(parts, 1)
        if guard is not None:
            parts = jnp.where(guard(source), parts, jnp.zeros_like(parts))
        return jnp.dot(turns, parts, preferred_element_type=jnp.float32)

    def combine_parts(both):
        second = pltpu.roll(both[window:], quarter, 1)
        return both[:window] + jnp.where(low_lanes, -second, second)

    def settle(value, offset):
        late = jnp.full((window - 8, LANES), offset, jnp.int32) >= 8
        value = jnp.where(late, value[8:], value[:-8])
        value = value.reshape(TILE_X // 8 + 1, 8, LANES)
        ahead = lax.rem(offset, 8)
        value = pltpu.roll(value, lax.rem(8 - ahead, 8), 1)
        value = jnp.where(row < 8 - ahead, value[:-1], value[1:])
        return value.reshape(TILE_X, LANES)

    def project(step, pick, chunks, guard=None):
        shift = jitter(step, pick)
        aligned, offset = lax.div(shift, SLAB), lax.rem(shift, SLAB)
        both = None
        for source in range(GROUP):
            for pulse in range(pulses):
                add = term(step, pick, chunks, source, pulse, aligned, guard)
                both = add if both is None else both + add
        return [
            settle(combine_parts(both[:, n * LANES : (n + 1) * LANES]), offset) for n in range(len(chunks))
        ]

    def send(step, pick, chunk, value):
        outgoing[step - 1, pick, chunk] = value.astype(jnp.bfloat16)
        pl.when(step > 1)(lambda: to_above(step, pick, chunk).start())
        pl.when(step == 1)(lambda: to_owner(pick, chunk).start())

    def begin(step, pick, chunks):
        @pl.when(reaches(step))
        def _():
            values = project(step, pick, chunks)

            @pl.when(has_below)
            def _():
                for chunk, value in zip(chunks, values):
                    held[step - 1, pick, chunk] = value

            @pl.when(jnp.logical_not(has_below))
            def _():
                for chunk, value in zip(chunks, values):
                    send(step, pick, chunk, value)

    def begin_farthest(pick):
        values = project(REACH, pick, every, lambda source: source > core + CORES * pick)
        for chunk, value in zip(every, values):
            send(REACH, pick, chunk, value)

    def combine(step, chunk):
        @pl.when(has_below & reaches(step))
        def _():
            @pl.loop(0, PAIR)
            def _(pick):
                to_above(step + 1, pick, chunk).wait_recv()
                value = held[step - 1, pick, chunk] + incoming[step - 1, pick, chunk].astype(jnp.float32)
                send(step, pick, chunk, value)

    def own_group():
        @pl.loop(0, PAIR)
        def _(turn):
            pick = lax.rem(1 - chip + turn, PAIR)
            values = project(0, pick, every, lambda source: source <= core + CORES * pick)

            @pl.when(turn == 0)
            def _():
                for chunk, value in zip(every, values):
                    across_out[chunk] = value.astype(jnp.bfloat16)
                    across(chunk).start()

            @pl.when(turn > 0)
            def _():
                for chunk, value in zip(every, values):
                    own[chunk] = value

    final_lanes = lax.broadcasted_iota(jnp.int32, (TILE_X, LANES), 1) < quarter

    def finish():
        for chunk in range(CHUNKS):
            across(chunk).wait_recv()
        for half in range(HALVES):
            for chunk in range(CHUNKS):
                mine, theirs = own[chunk], across_in[chunk].astype(jnp.float32)
                final[half, chunk] = jnp.where(chip == half, mine, theirs)

        @pl.when(has_below)
        def _():
            for chunk in range(CHUNKS):
                for half in range(HALVES):
                    from_below(half, chunk).wait_recv()
                    final[half, chunk] += arrived[half, chunk].astype(jnp.float32)

        for half in range(HALVES):
            one, two = final[half, 0], final[half, 1]
            cut = slice(half * LANES, (half + 1) * LANES)
            real = jnp.where(final_lanes, one, pltpu.roll(two, quarter, 1))
            imag = jnp.where(final_lanes, pltpu.roll(one, quarter, 1), two)
            image[0, :, cut] = real.astype(jnp.bfloat16)
            image[1, :, cut] = imag.astype(jnp.bfloat16)

    forward(0)
    fetch_anchors.wait()
    fetch_table.wait()
    for chunk in every:
        if chunk > 0:
            forward(chunk)
        collect(chunk)
        pl.loop(0, PAIR)(lambda pick: begin(REACH - 1, pick, (chunk,)))

    @pl.when(reaches(REACH))
    def _():
        pl.loop(0, PAIR)(begin_farthest)

    @pl.loop(0, (REACH - 2) * PAIR)
    def _(item):
        begin(REACH - 2 - item // PAIR, item % PAIR, every)

    combine(REACH - 2, 0)
    own_group()
    for chunk in every[1:]:
        combine(REACH - 2, chunk)
    for step in (REACH - 1, *range(REACH - 3, 0, -1)):
        for chunk in every:
            combine(step, chunk)
    finish()

    for chunk in range(CHUNKS):
        for pulse in range(pulses):
            to_side(chunk, pulse).wait_send()
            to_mate(chunk, pulse).wait_send()
            pass_on(chunk, pulse).wait_send()
        across(chunk).wait_send()
        for pick in range(PAIR):
            for step in range(2, REACH + 1):
                pl.when(reaches(step))(to_above(step, pick, chunk).wait_send)
            pl.when(has_above)(to_owner(pick, chunk).wait_send)


def local(count, echoes, integer_cell_displacement, fractional_level_label, steering, tile_anchor):
    pulses, bins = echoes.shape[1], echoes.shape[4]
    channels, beams = steering.shape[1:]
    spacing = TILE_X // pulses
    first = -JITTER - spacing * (pulses - 1)
    rows = TILE_X * (STEPS - 1) + spacing * (pulses - 1) + 2 * JITTER + TILE_X + SLAB
    table = jnp.asarray(phase_table(beams, pulses, first, rows))
    scalars = jnp.asarray(scalar_table())
    pair = (CHUNKS, pulses)
    dma = pltpu.SemaphoreType.DMA
    narrow = (TILE_X, LANES)
    return pl.pallas_call(
        functools.partial(image_kernel, count),
        out_shape=jax.ShapeDtypeStruct((2, TILE_X, bins), jnp.bfloat16),
        in_specs=[pl.BlockSpec(memory_space=pltpu.HBM)] * 7,
        out_specs=pl.BlockSpec(memory_space=pltpu.VMEM),
        scratch_shapes=[
            pltpu.SMEM(tile_anchor.shape, jnp.int32),
            pltpu.SMEM(integer_cell_displacement.shape, jnp.int32),
            pltpu.SMEM(fractional_level_label.shape, jnp.int32),
            pltpu.SMEM(scalars.shape, jnp.float32),
            pltpu.VMEM(echoes.shape, echoes.dtype),
            pltpu.VMEM(steering.shape, steering.dtype),
            pltpu.VMEM(table.shape, table.dtype),
            dma((6 + pulses,)),
            pltpu.VMEM((HALVES, channels, 2 * LANES), jnp.bfloat16),
            pltpu.VMEM((2, beams, channels), jnp.bfloat16),
            pltpu.VMEM((CHUNKS, pulses, beams, LANES), jnp.bfloat16),
            pltpu.VMEM((CHUNKS, GROUP, pulses, beams, LANES), jnp.bfloat16),
            pltpu.VMEM((REACH - 1, PAIR, CHUNKS, *narrow), jnp.float32),
            pltpu.VMEM((CHUNKS, *narrow), jnp.float32),
            pltpu.VMEM((HALVES, CHUNKS, *narrow), jnp.float32),
            pltpu.VMEM((REACH, PAIR, CHUNKS, *narrow), jnp.bfloat16),
            pltpu.VMEM((REACH - 1, PAIR, CHUNKS, *narrow), jnp.bfloat16),
            pltpu.VMEM((HALVES, CHUNKS, *narrow), jnp.bfloat16),
            pltpu.VMEM((CHUNKS, *narrow), jnp.bfloat16),
            pltpu.VMEM((CHUNKS, *narrow), jnp.bfloat16),
            dma(pair), dma(pair), dma(pair), dma(pair), dma(pair), dma(pair),
            dma((REACH - 1, PAIR, CHUNKS)), dma((REACH - 1, PAIR, CHUNKS)),
            dma((PAIR, CHUNKS)), dma((HALVES, CHUNKS)), dma((CHUNKS,)), dma((CHUNKS,)),
        ],
        compiler_params=pltpu.CompilerParams(
            collective_id=0, has_side_effects=True, vmem_limit_bytes=67_043_328
        ),
        name="image",
    )(tile_anchor, integer_cell_displacement, fractional_level_label, scalars, echoes, steering, table)


def solution(mesh):
    placed = (
        P(None, ("scene", "along"), None, None, None),
        P(("scene", "along"), None),
        P(("scene", "along"), None),
        P(),
        P("scene"),
    )
    return jax.shard_map(
        functools.partial(local, mesh.shape["along"]),
        mesh=mesh,
        in_specs=placed,
        out_specs=P(None, ("scene", "along"), None),
        check_vma=False,
    )
```

```python
import functools

import jax
import jax.numpy as jnp
import numpy as np
from jax import lax
from jax.experimental import pallas as pl
from jax.experimental.pallas import tpu as pltpu
from jax.sharding import PartitionSpec as P

TILE_X = 256
STEPS = 16
TAPS = 8
SHIFTS = 16
FRACTION_LEVELS = 16
QUAD = 4093
WAVE_FOURTHS = 37
LANES = 128
SLAB = 16
JITTER = TILE_X // 4
GROUP = 4
CORES = 2
PAIR = GROUP // CORES
REACH = STEPS // GROUP
HALVES = 2
CHUNKS = 2
CYCLE = 4 * FRACTION_LEVELS
MESH = pl.DeviceIdType.MESH


def scalar_table():
    shift = np.arange(TAPS)[None] - (TAPS // 2 - 1) - np.arange(FRACTION_LEVELS)[:, None] / FRACTION_LEVELS
    kernel = np.sinc(shift) * (0.54 + 0.46 * np.cos(np.pi * shift / (TAPS // 2)))
    theta = 2 * np.pi * np.arange(CYCLE) / CYCLE
    return np.concatenate([kernel.ravel(), np.cos(theta), np.sin(theta)]).astype(np.float32)


def phase_table(beams, pulses, first, rows):
    offset = np.mod(np.arange(first, first + rows, dtype=np.int64), QUAD)[:, None]
    beam = np.arange(beams, dtype=np.int64)[None]
    units = (offset * offset + beam * beam * offset + beam * offset * offset) % QUAD
    phi = 2 * np.pi * units / QUAD
    gain = (STEPS * pulses * beams) ** -0.5
    table = gain * np.concatenate([np.cos(phi), np.sin(phi)], 1)
    return table.reshape(rows // SLAB, SLAB, 2 * beams).astype(jnp.bfloat16)


def compensate(pulse, cells, levels, scalars, echoes, straight):
    _, _, transmitters, receivers, _ = echoes.shape
    lane = lax.broadcasted_iota(jnp.int32, (8, LANES), 1)
    stack = 2 * receivers // 8
    reach_back = SHIFTS // 2 + TAPS // 2 - 1
    hop = TAPS // 2
    stays = lax.broadcasted_iota(jnp.int32, (2 * receivers, LANES), 1) < LANES - hop

    def tall(value):
        return jnp.concatenate([value] * stack, 0)

    @pl.loop(0, transmitters, unroll=4)
    def _(sender):
        cell, level = cells[pulse, sender], levels[pulse, sender]
        units = lax.rem(WAVE_FOURTHS * (cell * FRACTION_LEVELS + level), CYCLE)
        cosine = scalars[FRACTION_LEVELS * TAPS + units]
        sine = scalars[FRACTION_LEVELS * TAPS + CYCLE + units]
        both = jnp.concatenate([echoes[0, pulse, sender], echoes[1, pulse, sender]], 0)
        both = both.astype(jnp.float32)
        first, second = both[:, :LANES], both[:, LANES:]
        near, far = [None, None], [None, None]
        for tap in range(hop):
            step = cell - reach_back + tap
            turned = [pltpu.roll(part, lax.rem(2 * LANES - step, LANES), 1) for part in (first, second)]
            spot = lane + step
            begun, not_over = spot >= 0, spot < LANES
            wide = tall(spot)
            swapped = (wide < 0) | (wide >= LANES)
            columns = (
                jnp.where(swapped, turned[1], turned[0]), jnp.where(swapped, turned[0], turned[1])
            )
            weight, later = scalars[level * TAPS + tap], scalars[level * TAPS + hop + tap]
            weights = [jnp.where(begun, weight, 0.0), jnp.where(not_over, weight, 0.0)]
            laters = [jnp.where(begun ^ (lane < hop), later, 0.0), jnp.where(not_over, later, 0.0)]
            for c, column in enumerate(columns):
                add, add_far = tall(weights[c]) * column, tall(laters[c]) * column
                near[c] = add if tap == 0 else near[c] + add
                far[c] = add_far if tap == 0 else far[c] + add_far
        ahead = [pltpu.roll(part, LANES - hop, 1) for part in far]
        sums = [
            near[0] + jnp.where(stays, ahead[0], ahead[1]), near[1] + jnp.where(stays, ahead[1], ahead[0])
        ]
        rows = pl.ds(pl.multiple_of(sender * receivers, receivers), receivers)
        for half in range(HALVES):
            a, b = sums[half][:receivers], sums[half][receivers:]
            straight[half, rows, :LANES] = (cosine * a + sine * b).astype(jnp.bfloat16)
            straight[half, rows, LANES:] = (cosine * b - sine * a).astype(jnp.bfloat16)


def image_kernel(
    count, far_anchors, far_cells, far_levels, far_scalars, far_echoes, far_steering, far_table, image,
    anchors, cells, levels, scalars, echoes, steering, table, fetched,
    straight, turned, outbox, got, held, own, final, outgoing, incoming, arrived, across_out, across_in,
    mate_send, mate_recv, side_send, side_recv, pass_send, pass_recv,
    up_send, up_recv, last_send, last_recv, across_send, across_recv,
):
    pulses = echoes.shape[1]
    beams = steering.shape[2]
    spacing = TILE_X // pulses
    window = TILE_X + SLAB
    quarter = LANES // CHUNKS
    pieces = [
        (far_cells, cells), (far_levels, levels), (far_scalars, scalars),
        *[(far_echoes.at[:, pulse], echoes.at[:, pulse]) for pulse in range(pulses)],
        (far_steering, steering), (far_anchors, anchors), (far_table, table),
    ]
    fetches = [
        pltpu.make_async_copy(source, landing, fetched.at[number])
        for number, (source, landing) in enumerate(pieces)
    ]
    for fetch in fetches:
        fetch.start()
    small, fetch_echoes = fetches[:3], fetches[3 : 3 + pulses]
    fetch_steering, fetch_anchors, fetch_table = fetches[3 + pulses :]
    me = lax.axis_index("along")
    group, place = me // GROUP, me % GROUP
    chip, core = place // CORES, place % CORES
    groups = count // GROUP
    mate_place, side_place = chip * CORES + 1 - core, (1 - chip) * CORES + core
    far_place = GROUP - 1 - place
    mate, side = group * GROUP + mate_place, group * GROUP + side_place
    has_below, has_above = group > 0, group < groups - 1

    barrier = pltpu.get_barrier_semaphore()

    def greet(other):
        pl.semaphore_signal(barrier, inc=1, device_id={"along": other}, device_id_type=MESH)

    greet(mate)
    greet(side)

    @pl.when(has_below)
    def _():
        greet(me - GROUP)
        greet(side - GROUP)

    @pl.when(has_above)
    def _():
        greet(me + GROUP)
        greet(side + GROUP)

    def remote(source, landing, send, recv, device):
        return pltpu.make_async_remote_copy(
            src_ref=source, dst_ref=landing, send_sem=send, recv_sem=recv,
            device_id={"along": device}, device_id_type=MESH,
        )

    def to_side(chunk, pulse):
        return remote(
            outbox.at[chunk, pulse], got.at[chunk, place, pulse],
            side_send.at[chunk, pulse], side_recv.at[chunk, pulse], side,
        )

    def to_mate(chunk, pulse):
        mine = got.at[chunk, place, pulse]
        return remote(mine, mine, mate_send.at[chunk, pulse], mate_recv.at[chunk, pulse], mate)

    def pass_on(chunk, pulse):
        theirs = got.at[chunk, side_place, pulse]
        return remote(theirs, theirs, pass_send.at[chunk, pulse], pass_recv.at[chunk, pulse], mate)

    def to_above(step, pick, chunk):
        return remote(
            outgoing.at[step - 1, pick, chunk], incoming.at[step - 2, pick, chunk],
            up_send.at[step - 2, pick, chunk], up_recv.at[step - 2, pick, chunk], me + GROUP,
        )

    def to_owner(pick, chunk):
        return remote(
            outgoing.at[0, pick, chunk], arrived.at[chip, chunk],
            last_send.at[pick, chunk], last_recv.at[chip, chunk],
            (group + 1) * GROUP + core + CORES * pick,
        )

    def from_below(half, chunk):
        return remote(
            arrived.at[half, chunk], arrived.at[half, chunk],
            last_send.at[half, chunk], last_recv.at[half, chunk], side,
        )

    def across(chunk):
        return remote(
            across_out.at[chunk], across_in.at[chunk], across_send.at[chunk], across_recv.at[chunk], side
        )

    every = tuple(range(CHUNKS))
    first_lanes = lax.broadcasted_iota(jnp.int32, (beams, LANES), 1) < quarter

    def form(pulse, half):
        one = jnp.dot(turned[0], straight[half], preferred_element_type=jnp.float32)
        two = jnp.dot(turned[1], straight[half], preferred_element_type=jnp.float32)
        real, imag = one[:, :LANES] - two[:, LANES:], one[:, LANES:] + two[:, :LANES]
        return (
            jnp.where(first_lanes, real, pltpu.roll(imag, quarter, 1)).astype(jnp.bfloat16),
            jnp.where(first_lanes, pltpu.roll(real, quarter, 1), imag).astype(jnp.bfloat16),
        )

    for pulse in range(pulses):
        if pulse == 0:
            for fetch in small:
                fetch.wait()
        fetch_echoes[pulse].wait()
        compensate(pulse, cells, levels, scalars, echoes, straight)
        if pulse == 0:
            fetch_steering.wait()
            turned[0] = steering[0].T
            turned[1] = steering[1].T
        for chunk, block in enumerate(form(pulse, 1 - chip)):
            outbox[chunk, pulse] = block
        if pulse == 0:
            pl.semaphore_wait(
                barrier, 2 + 2 * has_below.astype(jnp.int32) + 2 * has_above.astype(jnp.int32)
            )
        to_side(0, pulse).start()
        for chunk, block in enumerate(form(pulse, chip)):
            got[chunk, place, pulse] = block
        to_mate(0, pulse).start()
    for chunk in range(1, CHUNKS):
        for pulse in range(pulses):
            to_side(chunk, pulse).start()
            to_mate(chunk, pulse).start()

    def reaches(step):
        return group + step < groups

    def forward(chunk):
        for pulse in range(pulses):
            to_side(chunk, pulse).wait_recv()
            pass_on(chunk, pulse).start()

    def collect(chunk):
        for pulse in range(pulses):
            to_mate(chunk, pulse).wait_recv()
            pass_on(chunk, pulse).wait_recv()

    row = lax.broadcasted_iota(jnp.int32, (TILE_X // 8, 8, LANES), 1)
    low_lanes = lax.broadcasted_iota(jnp.int32, (window, LANES), 1) < quarter

    def jitter(step, pick):
        tile = (group + step) * GROUP + core + CORES * pick
        return jnp.clip(anchors[tile] - tile * TILE_X, -JITTER, JITTER) + JITTER

    def term(step, pick, chunks, source, pulse, aligned, guard):
        blocks = GROUP * step + core + CORES * pick - source
        if guard is not None:
            blocks = jnp.clip(blocks, 0, STEPS - 1)
        start = TILE_X // SLAB * blocks + spacing // SLAB * (pulses - 1 - pulse)
        slabs = pl.ds(start + aligned, window // SLAB)
        turns = [table[slabs, :, cut].reshape(window, beams) for cut in (slice(0, beams), slice(beams, 2 * beams))]
        turns = jnp.concatenate(turns, 0)
        parts = [got[chunk, source, pulse] for chunk in chunks]
        parts = parts[0] if len(parts) == 1 else jnp.concatenate(parts, 1)
        if guard is not None:
            parts = jnp.where(guard(source), parts, jnp.zeros_like(parts))
        return jnp.dot(turns, parts, preferred_element_type=jnp.float32)

    def combine_parts(both):
        second = pltpu.roll(both[window:], quarter, 1)
        return both[:window] + jnp.where(low_lanes, -second, second)

    def settle(value, offset):
        late = jnp.full((window - 8, LANES), offset, jnp.int32) >= 8
        value = jnp.where(late, value[8:], value[:-8])
        value = value.reshape(TILE_X // 8 + 1, 8, LANES)
        ahead = lax.rem(offset, 8)
        value = pltpu.roll(value, lax.rem(8 - ahead, 8), 1)
        value = jnp.where(row < 8 - ahead, value[:-1], value[1:])
        return value.reshape(TILE_X, LANES)

    def project(step, pick, chunks, guard=None):
        shift = jitter(step, pick)
        aligned, offset = lax.div(shift, SLAB), lax.rem(shift, SLAB)
        both = None
        for source in range(GROUP):
            for pulse in range(pulses):
                add = term(step, pick, chunks, source, pulse, aligned, guard)
                both = add if both is None else both + add
        return [
            settle(combine_parts(both[:, n * LANES : (n + 1) * LANES]), offset) for n in range(len(chunks))
        ]

    def send(step, pick, chunk, value):
        outgoing[step - 1, pick, chunk] = value.astype(jnp.bfloat16)
        pl.when(step > 1)(lambda: to_above(step, pick, chunk).start())
        pl.when(step == 1)(lambda: to_owner(pick, chunk).start())

    def begin(step, pick, chunks):
        @pl.when(reaches(step))
        def _():
            values = project(step, pick, chunks)

            @pl.when(has_below)
            def _():
                for chunk, value in zip(chunks, values):
                    held[step - 1, pick, chunk] = value

            @pl.when(jnp.logical_not(has_below))
            def _():
                for chunk, value in zip(chunks, values):
                    send(step, pick, chunk, value)

    def begin_farthest(pick):
        values = project(REACH, pick, every, lambda source: source > core + CORES * pick)
        for chunk, value in zip(every, values):
            send(REACH, pick, chunk, value)

    def combine(step, chunk):
        @pl.when(has_below & reaches(step))
        def _():
            @pl.loop(0, PAIR)
            def _(pick):
                to_above(step + 1, pick, chunk).wait_recv()
                value = held[step - 1, pick, chunk] + incoming[step - 1, pick, chunk].astype(jnp.float32)
                send(step, pick, chunk, value)

    def own_group():
        @pl.loop(0, PAIR)
        def _(turn):
            pick = lax.rem(1 - chip + turn, PAIR)
            values = project(0, pick, every, lambda source: source <= core + CORES * pick)

            @pl.when(turn == 0)
            def _():
                for chunk, value in zip(every, values):
                    across_out[chunk] = value.astype(jnp.bfloat16)
                    across(chunk).start()

            @pl.when(turn > 0)
            def _():
                for chunk, value in zip(every, values):
                    own[chunk] = value

    final_lanes = lax.broadcasted_iota(jnp.int32, (TILE_X, LANES), 1) < quarter

    def finish():
        for chunk in range(CHUNKS):
            across(chunk).wait_recv()
        for half in range(HALVES):
            for chunk in range(CHUNKS):
                mine, theirs = own[chunk], across_in[chunk].astype(jnp.float32)
                final[half, chunk] = jnp.where(chip == half, mine, theirs)

        @pl.when(has_below)
        def _():
            for chunk in range(CHUNKS):
                for half in range(HALVES):
                    from_below(half, chunk).wait_recv()
                    final[half, chunk] += arrived[half, chunk].astype(jnp.float32)

        for half in range(HALVES):
            one, two = final[half, 0], final[half, 1]
            cut = slice(half * LANES, (half + 1) * LANES)
            real = jnp.where(final_lanes, one, pltpu.roll(two, quarter, 1))
            imag = jnp.where(final_lanes, pltpu.roll(one, quarter, 1), two)
            image[0, :, cut] = real.astype(jnp.bfloat16)
            image[1, :, cut] = imag.astype(jnp.bfloat16)

    forward(0)
    fetch_anchors.wait()
    fetch_table.wait()
    for chunk in every:
        if chunk > 0:
            forward(chunk)
        collect(chunk)
        pl.loop(0, PAIR)(lambda pick: begin(REACH - 1, pick, (chunk,)))

    @pl.when(reaches(REACH))
    def _():
        pl.loop(0, PAIR)(begin_farthest)

    @pl.loop(0, (REACH - 2) * PAIR)
    def _(item):
        begin(REACH - 2 - item // PAIR, item % PAIR, every)

    combine(REACH - 2, 0)
    own_group()
    for chunk in every[1:]:
        combine(REACH - 2, chunk)
    for step in (REACH - 1, *range(REACH - 3, 0, -1)):
        for chunk in every:
            combine(step, chunk)
    finish()

    for chunk in range(CHUNKS):
        for pulse in range(pulses):
            to_side(chunk, pulse).wait_send()
            to_mate(chunk, pulse).wait_send()
            pass_on(chunk, pulse).wait_send()
        across(chunk).wait_send()
        for pick in range(PAIR):
            for step in range(2, REACH + 1):
                pl.when(reaches(step))(to_above(step, pick, chunk).wait_send)
            pl.when(has_above)(to_owner(pick, chunk).wait_send)


def local(count, echoes, integer_cell_displacement, fractional_level_label, steering, tile_anchor):
    pulses, bins = echoes.shape[1], echoes.shape[4]
    channels, beams = steering.shape[1:]
    spacing = TILE_X // pulses
    first = -JITTER - spacing * (pulses - 1)
    rows = TILE_X * (STEPS - 1) + spacing * (pulses - 1) + 2 * JITTER + TILE_X + SLAB
    table = jnp.asarray(phase_table(beams, pulses, first, rows))
    scalars = jnp.asarray(scalar_table())
    pair = (CHUNKS, pulses)
    dma = pltpu.SemaphoreType.DMA
    narrow = (TILE_X, LANES)
    return pl.pallas_call(
        functools.partial(image_kernel, count),
        out_shape=pltpu.VMEM((2, TILE_X, bins), jnp.bfloat16),
        in_specs=[pl.BlockSpec(memory_space=pltpu.HBM)] * 7,
        out_specs=pl.BlockSpec(memory_space=pltpu.VMEM),
        scratch_shapes=[
            pltpu.SMEM(tile_anchor.shape, jnp.int32),
            pltpu.SMEM(integer_cell_displacement.shape, jnp.int32),
            pltpu.SMEM(fractional_level_label.shape, jnp.int32),
            pltpu.SMEM(scalars.shape, jnp.float32),
            pltpu.VMEM(echoes.shape, echoes.dtype),
            pltpu.VMEM(steering.shape, steering.dtype),
            pltpu.VMEM(table.shape, table.dtype),
            dma((6 + pulses,)),
            pltpu.VMEM((HALVES, channels, 2 * LANES), jnp.bfloat16),
            pltpu.VMEM((2, beams, channels), jnp.bfloat16),
            pltpu.VMEM((CHUNKS, pulses, beams, LANES), jnp.bfloat16),
            pltpu.VMEM((CHUNKS, GROUP, pulses, beams, LANES), jnp.bfloat16),
            pltpu.VMEM((REACH - 1, PAIR, CHUNKS, *narrow), jnp.float32),
            pltpu.VMEM((CHUNKS, *narrow), jnp.float32),
            pltpu.VMEM((HALVES, CHUNKS, *narrow), jnp.float32),
            pltpu.VMEM((REACH, PAIR, CHUNKS, *narrow), jnp.bfloat16),
            pltpu.VMEM((REACH - 1, PAIR, CHUNKS, *narrow), jnp.bfloat16),
            pltpu.VMEM((HALVES, CHUNKS, *narrow), jnp.bfloat16),
            pltpu.VMEM((CHUNKS, *narrow), jnp.bfloat16),
            pltpu.VMEM((CHUNKS, *narrow), jnp.bfloat16),
            dma(pair), dma(pair), dma(pair), dma(pair), dma(pair), dma(pair),
            dma((REACH - 1, PAIR, CHUNKS)), dma((REACH - 1, PAIR, CHUNKS)),
            dma((PAIR, CHUNKS)), dma((HALVES, CHUNKS)), dma((CHUNKS,)), dma((CHUNKS,)),
        ],
        compiler_params=pltpu.CompilerParams(
            collective_id=0, has_side_effects=True, vmem_limit_bytes=66_781_184
        ),
        name="image",
    )(tile_anchor, integer_cell_displacement, fractional_level_label, scalars, echoes, steering, table)


def solution(mesh):
    placed = (
        P(None, ("scene", "along"), None, None, None),
        P(("scene", "along"), None),
        P(("scene", "along"), None),
        P(),
        P("scene"),
    )
    return jax.shard_map(
        functools.partial(local, mesh.shape["along"]),
        mesh=mesh,
        in_specs=placed,
        out_specs=P(None, ("scene", "along"), None),
        check_vma=False,
    )
```

```python
import functools

import jax
import jax.numpy as jnp
import numpy as np
from jax import lax
from jax.experimental import pallas as pl
from jax.experimental.pallas import tpu as pltpu
from jax.sharding import PartitionSpec as P

TILE_X = 256
STEPS = 16
TAPS = 8
SHIFTS = 16
FRACTION_LEVELS = 16
QUAD = 4093
WAVE_FOURTHS = 37
LANES = 128
SLAB = 16
JITTER = TILE_X // 4
GROUP = 4
CORES = 2
PAIR = GROUP // CORES
REACH = STEPS // GROUP
HALVES = 2
CHUNKS = 2
FIRST, LAST = 0, 1
CYCLE = 4 * FRACTION_LEVELS
MESH = pl.DeviceIdType.MESH


def scalar_table():
    shift = np.arange(TAPS)[None] - (TAPS // 2 - 1) - np.arange(FRACTION_LEVELS)[:, None] / FRACTION_LEVELS
    kernel = np.sinc(shift) * (0.54 + 0.46 * np.cos(np.pi * shift / (TAPS // 2)))
    theta = 2 * np.pi * np.arange(CYCLE) / CYCLE
    return np.concatenate([kernel.ravel(), np.cos(theta), np.sin(theta)]).astype(np.float32)


def phase_table(beams, pulses, first, rows):
    offset = np.mod(np.arange(first, first + rows, dtype=np.int64), QUAD)[:, None]
    beam = np.arange(beams, dtype=np.int64)[None]
    units = (offset * offset + beam * beam * offset + beam * offset * offset) % QUAD
    phi = 2 * np.pi * units / QUAD
    gain = (STEPS * pulses * beams) ** -0.5
    table = gain * np.concatenate([np.cos(phi), np.sin(phi)], 1)
    return table.reshape(rows // SLAB, SLAB, 2 * beams).astype(jnp.bfloat16)


def compensate(pulse, cells, levels, scalars, echoes, straight):
    _, _, transmitters, receivers, _ = echoes.shape
    lane = lax.broadcasted_iota(jnp.int32, (8, LANES), 1)
    stack = 2 * receivers // 8
    reach_back = SHIFTS // 2 + TAPS // 2 - 1
    hop = TAPS // 2
    stays = lax.broadcasted_iota(jnp.int32, (2 * receivers, LANES), 1) < LANES - hop

    def tall(value):
        return jnp.concatenate([value] * stack, 0)

    @pl.loop(0, transmitters, unroll=4)
    def _(sender):
        cell, level = cells[pulse, sender], levels[pulse, sender]
        units = lax.rem(WAVE_FOURTHS * (cell * FRACTION_LEVELS + level), CYCLE)
        cosine = scalars[FRACTION_LEVELS * TAPS + units]
        sine = scalars[FRACTION_LEVELS * TAPS + CYCLE + units]
        both = jnp.concatenate([echoes[0, pulse, sender], echoes[1, pulse, sender]], 0)
        both = both.astype(jnp.float32)
        first, second = both[:, :LANES], both[:, LANES:]
        near, far = [None, None], [None, None]
        for tap in range(hop):
            step = cell - reach_back + tap
            turned = [pltpu.roll(part, lax.rem(2 * LANES - step, LANES), 1) for part in (first, second)]
            spot = lane + step
            begun, not_over = spot >= 0, spot < LANES
            wide = tall(spot)
            swapped = (wide < 0) | (wide >= LANES)
            columns = (
                jnp.where(swapped, turned[1], turned[0]), jnp.where(swapped, turned[0], turned[1])
            )
            weight, later = scalars[level * TAPS + tap], scalars[level * TAPS + hop + tap]
            weights = [jnp.where(begun, weight, 0.0), jnp.where(not_over, weight, 0.0)]
            laters = [jnp.where(begun ^ (lane < hop), later, 0.0), jnp.where(not_over, later, 0.0)]
            for c, column in enumerate(columns):
                add, add_far = tall(weights[c]) * column, tall(laters[c]) * column
                near[c] = add if tap == 0 else near[c] + add
                far[c] = add_far if tap == 0 else far[c] + add_far
        ahead = [pltpu.roll(part, LANES - hop, 1) for part in far]
        sums = [
            near[0] + jnp.where(stays, ahead[0], ahead[1]), near[1] + jnp.where(stays, ahead[1], ahead[0])
        ]
        rows = pl.ds(pl.multiple_of(sender * receivers, receivers), receivers)
        for half in range(HALVES):
            a, b = sums[half][:receivers], sums[half][receivers:]
            straight[half, rows, :LANES] = (cosine * a + sine * b).astype(jnp.bfloat16)
            straight[half, rows, LANES:] = (cosine * b - sine * a).astype(jnp.bfloat16)


def image_kernel(
    count, far_anchors, far_cells, far_levels, far_scalars, far_echoes, far_steering, far_table, image,
    anchors, cells, levels, scalars, echoes, steering, table, fetched,
    straight, turned, outbox, got, below, held, own, final, outgoing, incoming, arrived, across_out, across_in,
    rise_send, rise_recv, share_send, share_recv, mate_send, mate_recv, side_send, side_recv, pass_send, pass_recv,
    up_send, up_recv, last_send, last_recv, across_send, across_recv,
):
    pulses = echoes.shape[1]
    beams = steering.shape[2]
    spacing = TILE_X // pulses
    window = TILE_X + SLAB
    quarter = LANES // CHUNKS
    pieces = [
        (far_cells, cells), (far_levels, levels), (far_scalars, scalars),
        *[(far_echoes.at[:, pulse], echoes.at[:, pulse]) for pulse in range(pulses)],
        (far_steering, steering), (far_anchors, anchors), (far_table, table),
    ]
    fetches = [
        pltpu.make_async_copy(source, landing, fetched.at[number])
        for number, (source, landing) in enumerate(pieces)
    ]
    for fetch in fetches:
        fetch.start()
    small, fetch_echoes = fetches[:3], fetches[3 : 3 + pulses]
    fetch_steering, fetch_anchors, fetch_table = fetches[3 + pulses :]
    me = lax.axis_index("along")
    group, place = me // GROUP, me % GROUP
    chip, core = place // CORES, place % CORES
    groups = count // GROUP
    mate_place, side_place = chip * CORES + 1 - core, (1 - chip) * CORES + core
    far_place = GROUP - 1 - place
    mate, side = group * GROUP + mate_place, group * GROUP + side_place
    has_below, has_above = group > 0, group < groups - 1
    lowest, second = group == 0, group == 1
    sooner = FIRST + (1 - 2 * FIRST) * lowest.astype(jnp.int32)
    order = (sooner, 1 - sooner)

    barrier = pltpu.get_barrier_semaphore()

    def greet(other):
        pl.semaphore_signal(barrier, inc=1, device_id={"along": other}, device_id_type=MESH)

    greet(mate)
    greet(side)

    @pl.when(has_below)
    def _():
        greet(me - GROUP)
        greet(side - GROUP)

    @pl.when(has_above)
    def _():
        greet(me + GROUP)
        greet(side + GROUP)

    def remote(source, landing, send, recv, device):
        return pltpu.make_async_remote_copy(
            src_ref=source, dst_ref=landing, send_sem=send, recv_sem=recv,
            device_id={"along": device}, device_id_type=MESH,
        )

    def to_side(chunk, pulse):
        return remote(
            outbox.at[chunk, pulse], got.at[chunk, place, pulse],
            side_send.at[chunk, pulse], side_recv.at[chunk, pulse], side,
        )

    def to_mate(chunk, pulse):
        mine = got.at[chunk, place, pulse]
        return remote(mine, mine, mate_send.at[chunk, pulse], mate_recv.at[chunk, pulse], mate)

    def pass_on(chunk, pulse):
        theirs = got.at[chunk, side_place, pulse]
        return remote(theirs, theirs, pass_send.at[chunk, pulse], pass_recv.at[chunk, pulse], mate)

    def rise(cross, pulse):
        return remote(
            outbox.at[FIRST, pulse] if cross else got.at[FIRST, place, pulse], below.at[place, pulse],
            rise_send.at[cross, pulse], rise_recv.at[cross, pulse], (side if cross else me) + GROUP,
        )

    def share(cross, pulse):
        risen = below.at[side_place if cross else place, pulse]
        return remote(risen, risen, share_send.at[cross, pulse], share_recv.at[cross, pulse], mate)

    def to_above(step, pick, chunk):
        return remote(
            outgoing.at[step - 1, pick, chunk], incoming.at[step - 2, pick, chunk],
            up_send.at[step - 2, pick, chunk], up_recv.at[step - 2, pick, chunk], me + GROUP,
        )

    def to_owner(pick, chunk):
        return remote(
            outgoing.at[0, pick, chunk], arrived.at[chip, chunk],
            last_send.at[pick, chunk], last_recv.at[chip, chunk],
            (group + 1) * GROUP + core + CORES * pick,
        )

    def from_below(half, chunk):
        return remote(
            arrived.at[half, chunk], arrived.at[half, chunk],
            last_send.at[half, chunk], last_recv.at[half, chunk], side,
        )

    def across(chunk):
        return remote(
            across_out.at[chunk], across_in.at[chunk], across_send.at[chunk], across_recv.at[chunk], side
        )

    every = tuple(range(CHUNKS))
    first_lanes = lax.broadcasted_iota(jnp.int32, (beams, LANES), 1) < quarter

    def form(pulse, half):
        one = jnp.dot(turned[0], straight[half], preferred_element_type=jnp.float32)
        two = jnp.dot(turned[1], straight[half], preferred_element_type=jnp.float32)
        real, imag = one[:, :LANES] - two[:, LANES:], one[:, LANES:] + two[:, :LANES]
        return (
            jnp.where(first_lanes, real, pltpu.roll(imag, quarter, 1)).astype(jnp.bfloat16),
            jnp.where(first_lanes, pltpu.roll(real, quarter, 1), imag).astype(jnp.bfloat16),
        )

    for pulse in range(pulses):
        if pulse == 0:
            for fetch in small:
                fetch.wait()
        fetch_echoes[pulse].wait()
        compensate(pulse, cells, levels, scalars, echoes, straight)
        if pulse == 0:
            fetch_steering.wait()
            turned[0] = steering[0].T
            turned[1] = steering[1].T
        for chunk, block in enumerate(form(pulse, 1 - chip)):
            outbox[chunk, pulse] = block
        if pulse == 0:
            pl.semaphore_wait(
                barrier, 2 + 2 * has_below.astype(jnp.int32) + 2 * has_above.astype(jnp.int32)
            )
        to_side(sooner, pulse).start()
        for chunk, block in enumerate(form(pulse, chip)):
            got[chunk, place, pulse] = block
        to_mate(sooner, pulse).start()
        pl.when(lowest & has_above)(rise(0, pulse).start)
    for pulse in range(pulses):
        pl.when(lowest & has_above)(rise(1, pulse).start)
    for pulse in range(pulses):
        to_side(order[1], pulse).start()
        to_mate(order[1], pulse).start()

    def reaches(step):
        return group + step < groups

    def forward(chunk):
        for pulse in range(pulses):
            to_side(chunk, pulse).wait_recv()
            pass_on(chunk, pulse).start()

    def collect(chunk):
        for pulse in range(pulses):
            to_mate(chunk, pulse).wait_recv()
            pass_on(chunk, pulse).wait_recv()

    row = lax.broadcasted_iota(jnp.int32, (TILE_X // 8, 8, LANES), 1)
    low_lanes = lax.broadcasted_iota(jnp.int32, (window, LANES), 1) < quarter

    def jitter(step, pick):
        tile = (group + step) * GROUP + core + CORES * pick
        return jnp.clip(anchors[tile] - tile * TILE_X, -JITTER, JITTER) + JITTER

    def beams_of(*chunks):
        def fetch(source, pulse):
            parts = [got[chunk, source, pulse] for chunk in chunks]
            return parts[0] if len(parts) == 1 else jnp.concatenate(parts, 1)

        return fetch

    def beams_below(source, pulse):
        return below[source, pulse]

    def term(step, pick, parts, source, pulse, aligned, guard):
        blocks = GROUP * step + core + CORES * pick - source
        if guard is not None:
            blocks = jnp.clip(blocks, 0, STEPS - 1)
            parts = jnp.where(guard(source), parts, jnp.zeros_like(parts))
        start = TILE_X // SLAB * blocks + spacing // SLAB * (pulses - 1 - pulse)
        slabs = pl.ds(start + aligned, window // SLAB)
        turns = [table[slabs, :, cut].reshape(window, beams) for cut in (slice(0, beams), slice(beams, 2 * beams))]
        return jnp.dot(jnp.concatenate(turns, 0), parts, preferred_element_type=jnp.float32)

    def combine_parts(both):
        second = pltpu.roll(both[window:], quarter, 1)
        return both[:window] + jnp.where(low_lanes, -second, second)

    def settle(value, offset):
        late = jnp.full((window - 8, LANES), offset, jnp.int32) >= 8
        value = jnp.where(late, value[8:], value[:-8])
        value = value.reshape(TILE_X // 8 + 1, 8, LANES)
        ahead = lax.rem(offset, 8)
        value = pltpu.roll(value, lax.rem(8 - ahead, 8), 1)
        value = jnp.where(row < 8 - ahead, value[:-1], value[1:])
        return value.reshape(TILE_X, LANES)

    def project(step, pick, fetch, guard=None, rises=0):
        shift = jitter(step, pick)
        aligned, offset = lax.div(shift, SLAB), lax.rem(shift, SLAB)
        both = None
        for source in range(GROUP):
            for pulse in range(pulses):
                parts = fetch(source, pulse)
                add = term(step + rises, pick, parts, source, pulse, aligned, guard)
                both = add if both is None else both + add
        return [
            settle(combine_parts(both[:, n : n + LANES]), offset) for n in range(0, both.shape[1], LANES)
        ]

    def beyond(pick):
        return lambda source: source > core + CORES * pick

    def within(pick):
        return lambda source: source <= core + CORES * pick

    def send(step, pick, chunk, value):
        outgoing[step - 1, pick, chunk] = value.astype(jnp.bfloat16)
        pl.when(step > 1)(lambda: to_above(step, pick, chunk).start())
        pl.when(step == 1)(lambda: to_owner(pick, chunk).start())

    def each_pick(active):
        def run(body):
            @pl.when(active)
            def _():
                pl.loop(0, PAIR)(body)

        return run

    def keep(step, pick, chunks, values):
        for chunk, value in zip(chunks, values):
            held[step - 1, pick, chunk] = value

    def add_below(step):
        @each_pick(second & reaches(step))
        def _(pick):
            guard = beyond(pick) if step + 1 == REACH else None
            (value,) = project(step, pick, beams_below, guard, 1)
            send(step, pick, FIRST, held[step - 1, pick, FIRST] + value)

    def combine(step, chunk):
        active = group > 1 if chunk == FIRST else has_below

        @each_pick(active & reaches(step))
        def _(pick):
            to_above(step + 1, pick, chunk).wait_recv()
            value = held[step - 1, pick, chunk] + incoming[step - 1, pick, chunk].astype(jnp.float32)
            send(step, pick, chunk, value)

    def own_group(active, rises):
        @each_pick(active)
        def _(turn):
            pick = lax.rem(1 - chip + turn, PAIR)
            values = project(0, pick, beams_of(*every), within(pick))
            if rises:
                values[FIRST] += project(0, pick, beams_below, None, 1)[0]

            @pl.when(turn == 0)
            def _():
                for chunk, value in zip(every, values):
                    across_out[chunk] = value.astype(jnp.bfloat16)
                    across(chunk).start()

            @pl.when(turn > 0)
            def _():
                for chunk, value in zip(every, values):
                    own[chunk] = value

    final_lanes = lax.broadcasted_iota(jnp.int32, (TILE_X, LANES), 1) < quarter

    def finish():
        for chunk in range(CHUNKS):
            across(chunk).wait_recv()
        for half in range(HALVES):
            for chunk in range(CHUNKS):
                mine, theirs = own[chunk], across_in[chunk].astype(jnp.float32)
                final[half, chunk] = jnp.where(chip == half, mine, theirs)

        for chunk in range(CHUNKS):

            @pl.when(group > 1 if chunk == FIRST else has_below)
            def _():
                for half in range(HALVES):
                    from_below(half, chunk).wait_recv()
                    final[half, chunk] += arrived[half, chunk].astype(jnp.float32)

        for half in range(HALVES):
            one, two = final[half, 0], final[half, 1]
            cut = slice(half * LANES, (half + 1) * LANES)
            real = jnp.where(final_lanes, one, pltpu.roll(two, quarter, 1))
            imag = jnp.where(final_lanes, pltpu.roll(one, quarter, 1), two)
            image[0, :, cut] = real.astype(jnp.bfloat16)
            image[1, :, cut] = imag.astype(jnp.bfloat16)

    forward(order[0])
    fetch_anchors.wait()
    fetch_table.wait()
    collect(order[0])

    @pl.when(lowest)
    def _():
        @pl.loop(0, (REACH - 1) * PAIR)
        def _(item):
            step, pick = REACH - 1 - item // PAIR, item % PAIR

            @pl.when(reaches(step))
            def _():
                send(step, pick, LAST, project(step, pick, beams_of(LAST))[0])

        @each_pick(reaches(REACH))
        def _(pick):
            send(REACH, pick, LAST, project(REACH, pick, beams_of(LAST), beyond(pick))[0])

    early = REACH - 2
    each_pick(has_below & reaches(early))(
        lambda pick: keep(early, pick, (FIRST,), project(early, pick, beams_of(FIRST)))
    )
    forward(order[1])
    collect(order[1])

    @pl.when(second)
    def _():
        for pulse in range(pulses):
            for cross in range(2):
                rise(cross, pulse).wait_recv()
                share(cross, pulse).start()
        for pulse in range(pulses):
            for cross in range(2):
                share(cross, pulse).wait_recv()

    add_below(early)
    each_pick(has_below & reaches(early))(
        lambda pick: keep(early, pick, (LAST,), project(early, pick, beams_of(LAST)))
    )

    @each_pick(has_below & reaches(REACH))
    def _(pick):
        for chunk, value in zip(every, project(REACH, pick, beams_of(*every), beyond(pick))):
            send(REACH, pick, chunk, value)

    for step in (early, REACH - 1, *range(early - 1, 0, -1)):
        if step != early:
            each_pick(has_below & reaches(step))(
                lambda pick: keep(step, pick, every, project(step, pick, beams_of(*every)))
            )
            add_below(step)
        if step == 1:
            own_group(jnp.logical_not(second), False)
        for chunk in (LAST, FIRST):
            combine(step, chunk)
    own_group(second, True)
    finish()

    for pulse in range(pulses):
        for chunk in every:
            to_side(chunk, pulse).wait_send()
            to_mate(chunk, pulse).wait_send()
            pass_on(chunk, pulse).wait_send()
        for cross in range(2):
            pl.when(lowest & has_above)(rise(cross, pulse).wait_send)
            pl.when(second)(share(cross, pulse).wait_send)
    for chunk in every:
        across(chunk).wait_send()
        active = has_below if chunk == FIRST else group >= 0
        for pick in range(PAIR):
            for step in range(2, REACH + 1):
                pl.when(active & reaches(step))(to_above(step, pick, chunk).wait_send)
            pl.when(active & has_above)(to_owner(pick, chunk).wait_send)


def local(count, echoes, integer_cell_displacement, fractional_level_label, steering, tile_anchor):
    pulses, bins = echoes.shape[1], echoes.shape[4]
    channels, beams = steering.shape[1:]
    spacing = TILE_X // pulses
    first = -JITTER - spacing * (pulses - 1)
    rows = TILE_X * (STEPS - 1) + spacing * (pulses - 1) + 2 * JITTER + TILE_X + SLAB
    table = jnp.asarray(phase_table(beams, pulses, first, rows))
    scalars = jnp.asarray(scalar_table())
    pair = (CHUNKS, pulses)
    dma = pltpu.SemaphoreType.DMA
    narrow = (TILE_X, LANES)
    return pl.pallas_call(
        functools.partial(image_kernel, count),
        out_shape=pltpu.VMEM((2, TILE_X, bins), jnp.bfloat16),
        in_specs=[pl.BlockSpec(memory_space=pltpu.HBM)] * 7,
        out_specs=pl.BlockSpec(memory_space=pltpu.VMEM),
        scratch_shapes=[
            pltpu.SMEM(tile_anchor.shape, jnp.int32),
            pltpu.SMEM(integer_cell_displacement.shape, jnp.int32),
            pltpu.SMEM(fractional_level_label.shape, jnp.int32),
            pltpu.SMEM(scalars.shape, jnp.float32),
            pltpu.VMEM(echoes.shape, echoes.dtype),
            pltpu.VMEM(steering.shape, steering.dtype),
            pltpu.VMEM(table.shape, table.dtype),
            dma((6 + pulses,)),
            pltpu.VMEM((HALVES, channels, 2 * LANES), jnp.bfloat16),
            pltpu.VMEM((2, beams, channels), jnp.bfloat16),
            pltpu.VMEM((CHUNKS, pulses, beams, LANES), jnp.bfloat16),
            pltpu.VMEM((CHUNKS, GROUP, pulses, beams, LANES), jnp.bfloat16),
            pltpu.VMEM((GROUP, pulses, beams, LANES), jnp.bfloat16),
            pltpu.VMEM((REACH - 1, PAIR, CHUNKS, *narrow), jnp.float32),
            pltpu.VMEM((CHUNKS, *narrow), jnp.float32),
            pltpu.VMEM((HALVES, CHUNKS, *narrow), jnp.float32),
            pltpu.VMEM((REACH, PAIR, CHUNKS, *narrow), jnp.bfloat16),
            pltpu.VMEM((REACH - 1, PAIR, CHUNKS, *narrow), jnp.bfloat16),
            pltpu.VMEM((HALVES, CHUNKS, *narrow), jnp.bfloat16),
            pltpu.VMEM((CHUNKS, *narrow), jnp.bfloat16),
            pltpu.VMEM((CHUNKS, *narrow), jnp.bfloat16),
            dma((2, pulses)), dma((2, pulses)), dma((2, pulses)), dma((2, pulses)),
            dma(pair), dma(pair), dma(pair), dma(pair), dma(pair), dma(pair),
            dma((REACH - 1, PAIR, CHUNKS)), dma((REACH - 1, PAIR, CHUNKS)),
            dma((PAIR, CHUNKS)), dma((HALVES, CHUNKS)), dma((CHUNKS,)), dma((CHUNKS,)),
        ],
        compiler_params=pltpu.CompilerParams(
            collective_id=0, has_side_effects=True, vmem_limit_bytes=66_781_184
        ),
        name="image",
    )(tile_anchor, integer_cell_displacement, fractional_level_label, scalars, echoes, steering, table)


def solution(mesh):
    placed = (
        P(None, ("scene", "along"), None, None, None),
        P(("scene", "along"), None),
        P(("scene", "along"), None),
        P(),
        P("scene"),
    )
    return jax.shard_map(
        functools.partial(local, mesh.shape["along"]),
        mesh=mesh,
        in_specs=placed,
        out_specs=P(None, ("scene", "along"), None),
        check_vma=False,
    )
```

```python
import functools

import jax
import jax.numpy as jnp
import numpy as np
from jax import lax
from jax.experimental import pallas as pl
from jax.experimental.pallas import tpu as pltpu
from jax.sharding import PartitionSpec as P

TILE_X = 256
STEPS = 16
TAPS = 8
SHIFTS = 16
FRACTION_LEVELS = 16
QUAD = 4093
WAVE_FOURTHS = 37
LANES = 128
SLAB = 16
JITTER = TILE_X // 4
GROUP = 4
CORES = 2
PAIR = GROUP // CORES
REACH = STEPS // GROUP
HALVES = 2
CHUNKS = 2
FIRST, LAST = 0, 1
CYCLE = 4 * FRACTION_LEVELS
MESH = pl.DeviceIdType.MESH


def scalar_table():
    shift = np.arange(TAPS)[None] - (TAPS // 2 - 1) - np.arange(FRACTION_LEVELS)[:, None] / FRACTION_LEVELS
    kernel = np.sinc(shift) * (0.54 + 0.46 * np.cos(np.pi * shift / (TAPS // 2)))
    theta = 2 * np.pi * np.arange(CYCLE) / CYCLE
    return np.concatenate([kernel.ravel(), np.cos(theta), np.sin(theta)]).astype(np.float32)


def phase_table(beams, pulses, first, rows):
    offset = np.mod(np.arange(first, first + rows, dtype=np.int64), QUAD)[:, None]
    beam = np.arange(beams, dtype=np.int64)[None]
    units = (offset * offset + beam * beam * offset + beam * offset * offset) % QUAD
    phi = 2 * np.pi * units / QUAD
    gain = (STEPS * pulses * beams) ** -0.5
    table = gain * np.concatenate([np.cos(phi), np.sin(phi)], 1)
    return table.reshape(rows // SLAB, SLAB, 2 * beams).astype(jnp.bfloat16)


def compensate(pulse, cells, levels, scalars, echoes, straight):
    _, _, transmitters, receivers, _ = echoes.shape
    lane = lax.broadcasted_iota(jnp.int32, (8, LANES), 1)
    stack = 2 * receivers // 8
    reach_back = SHIFTS // 2 + TAPS // 2 - 1
    hop = TAPS // 2
    stays = lax.broadcasted_iota(jnp.int32, (2 * receivers, LANES), 1) < LANES - hop

    def tall(value):
        return jnp.concatenate([value] * stack, 0)

    @pl.loop(0, transmitters, unroll=4)
    def _(sender):
        cell, level = cells[pulse, sender], levels[pulse, sender]
        units = lax.rem(WAVE_FOURTHS * (cell * FRACTION_LEVELS + level), CYCLE)
        cosine = scalars[FRACTION_LEVELS * TAPS + units]
        sine = scalars[FRACTION_LEVELS * TAPS + CYCLE + units]
        both = jnp.concatenate([echoes[0, pulse, sender], echoes[1, pulse, sender]], 0)
        both = both.astype(jnp.float32)
        first, second = both[:, :LANES], both[:, LANES:]
        near, far = [None, None], [None, None]
        for tap in range(hop):
            step = cell - reach_back + tap
            turned = [pltpu.roll(part, lax.rem(2 * LANES - step, LANES), 1) for part in (first, second)]
            spot = lane + step
            begun, not_over = spot >= 0, spot < LANES
            wide = tall(spot)
            swapped = (wide < 0) | (wide >= LANES)
            columns = (
                jnp.where(swapped, turned[1], turned[0]), jnp.where(swapped, turned[0], turned[1])
            )
            weight, later = scalars[level * TAPS + tap], scalars[level * TAPS + hop + tap]
            weights = [jnp.where(begun, weight, 0.0), jnp.where(not_over, weight, 0.0)]
            laters = [jnp.where(begun ^ (lane < hop), later, 0.0), jnp.where(not_over, later, 0.0)]
            for c, column in enumerate(columns):
                add, add_far = tall(weights[c]) * column, tall(laters[c]) * column
                near[c] = add if tap == 0 else near[c] + add
                far[c] = add_far if tap == 0 else far[c] + add_far
        ahead = [pltpu.roll(part, LANES - hop, 1) for part in far]
        sums = [
            near[0] + jnp.where(stays, ahead[0], ahead[1]), near[1] + jnp.where(stays, ahead[1], ahead[0])
        ]
        rows = pl.ds(pl.multiple_of(sender * receivers, receivers), receivers)
        for half in range(HALVES):
            a, b = sums[half][:receivers], sums[half][receivers:]
            straight[pulse, half, rows, :LANES] = (cosine * a + sine * b).astype(jnp.bfloat16)
            straight[pulse, half, rows, LANES:] = (cosine * b - sine * a).astype(jnp.bfloat16)


def image_kernel(
    count, far_anchors, far_cells, far_levels, far_scalars, far_echoes, far_steering, far_table, image,
    anchors, cells, levels, scalars, echoes, steering, table, fetched,
    straight, turned, outbox, got, below, held, own, final, outgoing, incoming, arrived, across_out, across_in,
    rise_send, rise_recv, share_send, share_recv, mate_send, mate_recv, side_send, side_recv, pass_send, pass_recv,
    up_send, up_recv, last_send, last_recv, across_send, across_recv,
):
    pulses = echoes.shape[1]
    beams = steering.shape[2]
    spacing = TILE_X // pulses
    window = TILE_X + SLAB
    quarter = LANES // CHUNKS
    pieces = [
        (far_cells, cells), (far_levels, levels), (far_scalars, scalars),
        (far_steering, steering),
        *[(far_echoes.at[:, pulse], echoes.at[:, pulse]) for pulse in range(pulses)],
        (far_anchors, anchors), (far_table, table),
    ]
    fetches = [
        pltpu.make_async_copy(source, landing, fetched.at[number])
        for number, (source, landing) in enumerate(pieces)
    ]
    for fetch in fetches:
        fetch.start()
    small, fetch_steering, fetch_echoes = fetches[:3], fetches[3], fetches[4 : 4 + pulses]
    fetch_anchors, fetch_table = fetches[4 + pulses :]
    me = lax.axis_index("along")
    group, place = me // GROUP, me % GROUP
    chip, core = place // CORES, place % CORES
    groups = count // GROUP
    mate_place, side_place = chip * CORES + 1 - core, (1 - chip) * CORES + core
    far_place = GROUP - 1 - place
    mate, side = group * GROUP + mate_place, group * GROUP + side_place
    has_below, has_above = group > 0, group < groups - 1
    lowest, second = group == 0, group == 1

    barrier = pltpu.get_barrier_semaphore()

    def greet(other):
        pl.semaphore_signal(barrier, inc=1, device_id={"along": other}, device_id_type=MESH)

    greet(mate)
    greet(side)

    @pl.when(has_below)
    def _():
        greet(me - GROUP)
        greet(side - GROUP)

    @pl.when(has_above)
    def _():
        greet(me + GROUP)
        greet(side + GROUP)

    def remote(source, landing, send, recv, device):
        return pltpu.make_async_remote_copy(
            src_ref=source, dst_ref=landing, send_sem=send, recv_sem=recv,
            device_id={"along": device}, device_id_type=MESH,
        )

    def to_side(chunk, pulse):
        return remote(
            outbox.at[chunk, pulse], got.at[chunk, place, pulse],
            side_send.at[chunk, pulse], side_recv.at[chunk, pulse], side,
        )

    def to_mate(chunk, pulse):
        mine = got.at[chunk, place, pulse]
        return remote(mine, mine, mate_send.at[chunk, pulse], mate_recv.at[chunk, pulse], mate)

    def pass_on(chunk, pulse):
        theirs = got.at[chunk, side_place, pulse]
        return remote(theirs, theirs, pass_send.at[chunk, pulse], pass_recv.at[chunk, pulse], mate)

    def risen_place(cross):
        return side_place if cross else place

    def rise(cross, pulse):
        return remote(
            got.at[FIRST, risen_place(cross), pulse], below.at[risen_place(cross), pulse],
            rise_send.at[cross, pulse], rise_recv.at[cross, pulse], me + GROUP,
        )

    def share(cross, pulse):
        risen = below.at[risen_place(cross), pulse]
        return remote(risen, risen, share_send.at[cross, pulse], share_recv.at[cross, pulse], mate)

    def to_above(step, pick, chunk):
        return remote(
            outgoing.at[step - 1, pick, chunk], incoming.at[step - 2, pick, chunk],
            up_send.at[step - 2, pick, chunk], up_recv.at[step - 2, pick, chunk], me + GROUP,
        )

    def to_owner(pick, chunk):
        return remote(
            outgoing.at[0, pick, chunk], arrived.at[chip, chunk],
            last_send.at[pick, chunk], last_recv.at[chip, chunk],
            (group + 1) * GROUP + core + CORES * pick,
        )

    def from_below(half, chunk):
        return remote(
            arrived.at[half, chunk], arrived.at[half, chunk],
            last_send.at[half, chunk], last_recv.at[half, chunk], side,
        )

    def across(chunk):
        return remote(
            across_out.at[chunk], across_in.at[chunk], across_send.at[chunk], across_recv.at[chunk], side
        )

    every = tuple(range(CHUNKS))
    first_lanes = lax.broadcasted_iota(jnp.int32, (beams, LANES), 1) < quarter

    def form(pulse, half):
        one = jnp.dot(turned[0], straight[pulse, half], preferred_element_type=jnp.float32)
        two = jnp.dot(turned[1], straight[pulse, half], preferred_element_type=jnp.float32)
        real, imag = one[:, :LANES] - two[:, LANES:], one[:, LANES:] + two[:, :LANES]
        return (
            jnp.where(first_lanes, real, pltpu.roll(imag, quarter, 1)).astype(jnp.bfloat16),
            jnp.where(first_lanes, pltpu.roll(real, quarter, 1), imag).astype(jnp.bfloat16),
        )

    fetch_steering.wait()
    turned[0] = steering[0].T
    turned[1] = steering[1].T
    for pulse in range(pulses):
        if pulse == 0:
            for fetch in small:
                fetch.wait()
        fetch_echoes[pulse].wait()
        compensate(pulse, cells, levels, scalars, echoes, straight)
        for chunk, block in enumerate(form(pulse, 1 - chip)):
            outbox[chunk, pulse] = block
        if pulse == 0:
            pl.semaphore_wait(
                barrier, 2 + 2 * has_below.astype(jnp.int32) + 2 * has_above.astype(jnp.int32)
            )
        to_side(FIRST, pulse).start()
    for pulse in range(pulses):
        for chunk, block in enumerate(form(pulse, chip)):
            got[chunk, place, pulse] = block
        to_mate(FIRST, pulse).start()
        pl.when(lowest & has_above)(rise(0, pulse).start)
    for pulse in range(pulses):
        to_side(LAST, pulse).start()
        to_mate(LAST, pulse).start()

    def reaches(step):
        return group + step < groups

    def forward(chunk):
        for pulse in range(pulses):
            to_side(chunk, pulse).wait_recv()
            pass_on(chunk, pulse).start()
            if chunk == FIRST:
                pl.when(lowest & has_above)(rise(1, pulse).start)

    def collect(chunk):
        for pulse in range(pulses):
            to_mate(chunk, pulse).wait_recv()
            pass_on(chunk, pulse).wait_recv()

    row = lax.broadcasted_iota(jnp.int32, (TILE_X // 8, 8, LANES), 1)
    low_lanes = lax.broadcasted_iota(jnp.int32, (window, LANES), 1) < quarter

    def jitter(step, pick):
        tile = (group + step) * GROUP + core + CORES * pick
        return jnp.clip(anchors[tile] - tile * TILE_X, -JITTER, JITTER) + JITTER

    def beams_of(*chunks):
        def fetch(source, pulse):
            parts = [got[chunk, source, pulse] for chunk in chunks]
            return parts[0] if len(parts) == 1 else jnp.concatenate(parts, 1)

        return fetch

    def beams_below(source, pulse):
        return below[source, pulse]

    def term(step, pick, parts, source, pulse, aligned, guard):
        blocks = GROUP * step + core + CORES * pick - source
        if guard is not None:
            blocks = jnp.clip(blocks, 0, STEPS - 1)
            parts = jnp.where(guard(source), parts, jnp.zeros_like(parts))
        start = TILE_X // SLAB * blocks + spacing // SLAB * (pulses - 1 - pulse)
        slabs = pl.ds(start + aligned, window // SLAB)
        turns = [table[slabs, :, cut].reshape(window, beams) for cut in (slice(0, beams), slice(beams, 2 * beams))]
        return jnp.dot(jnp.concatenate(turns, 0), parts, preferred_element_type=jnp.float32)

    def combine_parts(both):
        second = pltpu.roll(both[window:], quarter, 1)
        return both[:window] + jnp.where(low_lanes, -second, second)

    def settle(value, offset):
        late = jnp.full((window - 8, LANES), offset, jnp.int32) >= 8
        value = jnp.where(late, value[8:], value[:-8])
        value = value.reshape(TILE_X // 8 + 1, 8, LANES)
        ahead = lax.rem(offset, 8)
        value = pltpu.roll(value, lax.rem(8 - ahead, 8), 1)
        value = jnp.where(row < 8 - ahead, value[:-1], value[1:])
        return value.reshape(TILE_X, LANES)

    def project(step, pick, fetch, guard=None, rises=0):
        shift = jitter(step, pick)
        aligned, offset = lax.div(shift, SLAB), lax.rem(shift, SLAB)
        both = None
        for source in range(GROUP):
            for pulse in range(pulses):
                parts = fetch(source, pulse)
                add = term(step + rises, pick, parts, source, pulse, aligned, guard)
                both = add if both is None else both + add
        return [
            settle(combine_parts(both[:, n : n + LANES]), offset) for n in range(0, both.shape[1], LANES)
        ]

    def beyond(pick):
        return lambda source: source > core + CORES * pick

    def within(pick):
        return lambda source: source <= core + CORES * pick

    def send(step, pick, chunk, value):
        outgoing[step - 1, pick, chunk] = value.astype(jnp.bfloat16)
        pl.when(step > 1)(lambda: to_above(step, pick, chunk).start())
        pl.when(step == 1)(lambda: to_owner(pick, chunk).start())

    def each_pick(active):
        def run(body):
            @pl.when(active)
            def _():
                pl.loop(0, PAIR)(body)

        return run

    def keep(step, pick, chunks, values):
        for chunk, value in zip(chunks, values):
            held[step - 1, pick, chunk] = value

    def add_below(step):
        @each_pick(second & reaches(step))
        def _(pick):
            guard = beyond(pick) if step + 1 == REACH else None
            (value,) = project(step, pick, beams_below, guard, 1)
            send(step, pick, FIRST, held[step - 1, pick, FIRST] + value)

    def combine(step, chunk):
        active = group > 1 if chunk == FIRST else has_below

        @each_pick(active & reaches(step))
        def _(pick):
            to_above(step + 1, pick, chunk).wait_recv()
            value = held[step - 1, pick, chunk] + incoming[step - 1, pick, chunk].astype(jnp.float32)
            send(step, pick, chunk, value)

    def own_group(active, rises):
        @each_pick(active)
        def _(turn):
            pick = lax.rem(1 - chip + turn, PAIR)
            values = project(0, pick, beams_of(*every), within(pick))
            if rises:
                values[FIRST] += project(0, pick, beams_below, None, 1)[0]

            @pl.when(turn == 0)
            def _():
                for chunk, value in zip(every, values):
                    across_out[chunk] = value.astype(jnp.bfloat16)
                    across(chunk).start()

            @pl.when(turn > 0)
            def _():
                for chunk, value in zip(every, values):
                    own[chunk] = value

    final_lanes = lax.broadcasted_iota(jnp.int32, (TILE_X, LANES), 1) < quarter

    def finish():
        for chunk in range(CHUNKS):
            across(chunk).wait_recv()
        for half in range(HALVES):
            for chunk in range(CHUNKS):
                mine, theirs = own[chunk], across_in[chunk].astype(jnp.float32)
                final[half, chunk] = jnp.where(chip == half, mine, theirs)

        for chunk in range(CHUNKS):

            @pl.when(group > 1 if chunk == FIRST else has_below)
            def _():
                for half in range(HALVES):
                    from_below(half, chunk).wait_recv()
                    final[half, chunk] += arrived[half, chunk].astype(jnp.float32)

        for half in range(HALVES):
            one, two = final[half, 0], final[half, 1]
            cut = slice(half * LANES, (half + 1) * LANES)
            real = jnp.where(final_lanes, one, pltpu.roll(two, quarter, 1))
            imag = jnp.where(final_lanes, pltpu.roll(one, quarter, 1), two)
            image[0, :, cut] = real.astype(jnp.bfloat16)
            image[1, :, cut] = imag.astype(jnp.bfloat16)

    forward(FIRST)
    fetch_anchors.wait()
    fetch_table.wait()
    collect(FIRST)
    early = REACH - 2
    each_pick(has_below & reaches(early))(
        lambda pick: keep(early, pick, (FIRST,), project(early, pick, beams_of(FIRST)))
    )
    forward(LAST)
    collect(LAST)

    @pl.when(lowest)
    def _():
        @pl.loop(0, (REACH - 1) * PAIR)
        def _(item):
            step, pick = REACH - 1 - item // PAIR, item % PAIR

            @pl.when(reaches(step))
            def _():
                send(step, pick, LAST, project(step, pick, beams_of(LAST))[0])

        @each_pick(reaches(REACH))
        def _(pick):
            send(REACH, pick, LAST, project(REACH, pick, beams_of(LAST), beyond(pick))[0])

    @pl.when(second)
    def _():
        for pulse in range(pulses):
            for cross in range(2):
                rise(cross, pulse).wait_recv()
                share(cross, pulse).start()
        for pulse in range(pulses):
            for cross in range(2):
                share(cross, pulse).wait_recv()

    add_below(early)
    each_pick(has_below & reaches(early))(
        lambda pick: keep(early, pick, (LAST,), project(early, pick, beams_of(LAST)))
    )

    @each_pick(has_below & reaches(REACH))
    def _(pick):
        for chunk, value in zip(every, project(REACH, pick, beams_of(*every), beyond(pick))):
            send(REACH, pick, chunk, value)

    for step in (early, REACH - 1, *range(early - 1, 0, -1)):
        if step != early:
            each_pick(has_below & reaches(step))(
                lambda pick: keep(step, pick, every, project(step, pick, beams_of(*every)))
            )
            add_below(step)
        if step == 1:
            own_group(jnp.logical_not(second), False)
        for chunk in (LAST, FIRST):
            combine(step, chunk)
    own_group(second, True)
    finish()

    for pulse in range(pulses):
        for chunk in every:
            to_side(chunk, pulse).wait_send()
            to_mate(chunk, pulse).wait_send()
            pass_on(chunk, pulse).wait_send()
        for cross in range(2):
            pl.when(lowest & has_above)(rise(cross, pulse).wait_send)
            pl.when(second)(share(cross, pulse).wait_send)
    for chunk in every:
        across(chunk).wait_send()
        active = has_below if chunk == FIRST else group >= 0
        for pick in range(PAIR):
            for step in range(2, REACH + 1):
                pl.when(active & reaches(step))(to_above(step, pick, chunk).wait_send)
            pl.when(active & has_above)(to_owner(pick, chunk).wait_send)


def local(count, echoes, integer_cell_displacement, fractional_level_label, steering, tile_anchor):
    pulses, bins = echoes.shape[1], echoes.shape[4]
    channels, beams = steering.shape[1:]
    spacing = TILE_X // pulses
    first = -JITTER - spacing * (pulses - 1)
    rows = TILE_X * (STEPS - 1) + spacing * (pulses - 1) + 2 * JITTER + TILE_X + SLAB
    table = jnp.asarray(phase_table(beams, pulses, first, rows))
    scalars = jnp.asarray(scalar_table())
    pair = (CHUNKS, pulses)
    dma = pltpu.SemaphoreType.DMA
    narrow = (TILE_X, LANES)
    return pl.pallas_call(
        functools.partial(image_kernel, count),
        out_shape=pltpu.VMEM((2, TILE_X, bins), jnp.bfloat16),
        in_specs=[pl.BlockSpec(memory_space=pltpu.HBM)] * 7,
        out_specs=pl.BlockSpec(memory_space=pltpu.VMEM),
        scratch_shapes=[
            pltpu.SMEM(tile_anchor.shape, jnp.int32),
            pltpu.SMEM(integer_cell_displacement.shape, jnp.int32),
            pltpu.SMEM(fractional_level_label.shape, jnp.int32),
            pltpu.SMEM(scalars.shape, jnp.float32),
            pltpu.VMEM(echoes.shape, echoes.dtype),
            pltpu.VMEM(steering.shape, steering.dtype),
            pltpu.VMEM(table.shape, table.dtype),
            dma((6 + pulses,)),
            pltpu.VMEM((pulses, HALVES, channels, 2 * LANES), jnp.bfloat16),
            pltpu.VMEM((2, beams, channels), jnp.bfloat16),
            pltpu.VMEM((CHUNKS, pulses, beams, LANES), jnp.bfloat16),
            pltpu.VMEM((CHUNKS, GROUP, pulses, beams, LANES), jnp.bfloat16),
            pltpu.VMEM((GROUP, pulses, beams, LANES), jnp.bfloat16),
            pltpu.VMEM((REACH - 1, PAIR, CHUNKS, *narrow), jnp.float32),
            pltpu.VMEM((CHUNKS, *narrow), jnp.float32),
            pltpu.VMEM((HALVES, CHUNKS, *narrow), jnp.float32),
            pltpu.VMEM((REACH, PAIR, CHUNKS, *narrow), jnp.bfloat16),
            pltpu.VMEM((REACH - 1, PAIR, CHUNKS, *narrow), jnp.bfloat16),
            pltpu.VMEM((HALVES, CHUNKS, *narrow), jnp.bfloat16),
            pltpu.VMEM((CHUNKS, *narrow), jnp.bfloat16),
            pltpu.VMEM((CHUNKS, *narrow), jnp.bfloat16),
            dma((2, pulses)), dma((2, pulses)), dma((2, pulses)), dma((2, pulses)),
            dma(pair), dma(pair), dma(pair), dma(pair), dma(pair), dma(pair),
            dma((REACH - 1, PAIR, CHUNKS)), dma((REACH - 1, PAIR, CHUNKS)),
            dma((PAIR, CHUNKS)), dma((HALVES, CHUNKS)), dma((CHUNKS,)), dma((CHUNKS,)),
        ],
        compiler_params=pltpu.CompilerParams(
            collective_id=0, has_side_effects=True, vmem_limit_bytes=66_781_184
        ),
        name="image",
    )(tile_anchor, integer_cell_displacement, fractional_level_label, scalars, echoes, steering, table)


def solution(mesh):
    placed = (
        P(None, ("scene", "along"), None, None, None),
        P(("scene", "along"), None),
        P(("scene", "along"), None),
        P(),
        P("scene"),
    )
    return jax.shard_map(
        functools.partial(local, mesh.shape["along"]),
        mesh=mesh,
        in_specs=placed,
        out_specs=P(None, ("scene", "along"), None),
        check_vma=False,
    )
```

```python
import functools

import jax
import jax.numpy as jnp
import numpy as np
from jax import lax
from jax.experimental import pallas as pl
from jax.experimental.pallas import tpu as pltpu
from jax.sharding import PartitionSpec as P

TILE_X = 256
STEPS = 16
TAPS = 8
SHIFTS = 16
FRACTION_LEVELS = 16
QUAD = 4093
WAVE_FOURTHS = 37
LANES = 128
SLAB = 16
JITTER = TILE_X // 4
GROUP = 4
CORES = 2
PAIR = GROUP // CORES
REACH = STEPS // GROUP
HALVES = 2
CHUNKS = 2
FIRST, LAST = 0, 1
CYCLE = 4 * FRACTION_LEVELS
MESH = pl.DeviceIdType.MESH


def scalar_table():
    shift = np.arange(TAPS)[None] - (TAPS // 2 - 1) - np.arange(FRACTION_LEVELS)[:, None] / FRACTION_LEVELS
    kernel = np.sinc(shift) * (0.54 + 0.46 * np.cos(np.pi * shift / (TAPS // 2)))
    theta = 2 * np.pi * np.arange(CYCLE) / CYCLE
    return np.concatenate([kernel.ravel(), np.cos(theta), np.sin(theta)]).astype(np.float32)


def phase_table(beams, pulses, first, rows):
    offset = np.mod(np.arange(first, first + rows, dtype=np.int64), QUAD)[:, None]
    beam = np.arange(beams, dtype=np.int64)[None]
    units = (offset * offset + beam * beam * offset + beam * offset * offset) % QUAD
    phi = 2 * np.pi * units / QUAD
    gain = (STEPS * pulses * beams) ** -0.5
    table = gain * np.concatenate([np.cos(phi), np.sin(phi)], 1)
    return table.reshape(rows // SLAB, SLAB, 2 * beams).astype(jnp.bfloat16)


def compensate(pulse, cells, levels, scalars, echoes, straight):
    _, _, transmitters, receivers, _ = echoes.shape
    lane = lax.broadcasted_iota(jnp.int32, (8, LANES), 1)
    stack = 2 * receivers // 8
    reach_back = SHIFTS // 2 + TAPS // 2 - 1
    hop = TAPS // 2
    stays = lax.broadcasted_iota(jnp.int32, (2 * receivers, LANES), 1) < LANES - hop

    def tall(value):
        return jnp.concatenate([value] * stack, 0)

    @pl.loop(0, transmitters, unroll=4)
    def _(sender):
        cell, level = cells[pulse, sender], levels[pulse, sender]
        units = lax.rem(WAVE_FOURTHS * (cell * FRACTION_LEVELS + level), CYCLE)
        cosine = scalars[FRACTION_LEVELS * TAPS + units]
        sine = scalars[FRACTION_LEVELS * TAPS + CYCLE + units]
        both = jnp.concatenate([echoes[0, pulse, sender], echoes[1, pulse, sender]], 0)
        both = both.astype(jnp.float32)
        first, second = both[:, :LANES], both[:, LANES:]
        near, far = [None, None], [None, None]
        for tap in range(hop):
            step = cell - reach_back + tap
            turned = [pltpu.roll(part, lax.rem(2 * LANES - step, LANES), 1) for part in (first, second)]
            spot = lane + step
            begun, not_over = spot >= 0, spot < LANES
            wide = tall(spot)
            swapped = (wide < 0) | (wide >= LANES)
            columns = (
                jnp.where(swapped, turned[1], turned[0]), jnp.where(swapped, turned[0], turned[1])
            )
            weight, later = scalars[level * TAPS + tap], scalars[level * TAPS + hop + tap]
            weights = [jnp.where(begun, weight, 0.0), jnp.where(not_over, weight, 0.0)]
            laters = [jnp.where(begun ^ (lane < hop), later, 0.0), jnp.where(not_over, later, 0.0)]
            for c, column in enumerate(columns):
                add, add_far = tall(weights[c]) * column, tall(laters[c]) * column
                near[c] = add if tap == 0 else near[c] + add
                far[c] = add_far if tap == 0 else far[c] + add_far
        ahead = [pltpu.roll(part, LANES - hop, 1) for part in far]
        sums = [
            near[0] + jnp.where(stays, ahead[0], ahead[1]), near[1] + jnp.where(stays, ahead[1], ahead[0])
        ]
        rows = pl.ds(pl.multiple_of(sender * receivers, receivers), receivers)
        for half in range(HALVES):
            a, b = sums[half][:receivers], sums[half][receivers:]
            straight[pulse, half, rows, :LANES] = (cosine * a + sine * b).astype(jnp.bfloat16)
            straight[pulse, half, rows, LANES:] = (cosine * b - sine * a).astype(jnp.bfloat16)


def image_kernel(
    count, far_anchors, far_cells, far_levels, far_scalars, far_echoes, far_steering, far_table, image,
    anchors, cells, levels, scalars, echoes, steering, table, fetched,
    straight, turned, outbox, got, below, held, own, final, outgoing, incoming, arrived, across_out, across_in,
    rise_send, rise_recv, share_send, share_recv, mate_send, mate_recv, side_send, side_recv, pass_send, pass_recv,
    up_send, up_recv, last_send, last_recv, across_send, across_recv,
):
    pulses = echoes.shape[1]
    beams = steering.shape[2]
    spacing = TILE_X // pulses
    window = TILE_X + SLAB
    quarter = LANES // CHUNKS
    pieces = [
        (far_cells, cells), (far_levels, levels), (far_scalars, scalars),
        (far_steering, steering),
        *[(far_echoes.at[:, pulse], echoes.at[:, pulse]) for pulse in range(pulses)],
        (far_anchors, anchors), (far_table, table),
    ]
    fetches = [
        pltpu.make_async_copy(source, landing, fetched.at[number])
        for number, (source, landing) in enumerate(pieces)
    ]
    small, fetch_steering, fetch_echoes = fetches[:3], fetches[3], fetches[4 : 4 + pulses]
    fetch_anchors, fetch_table = fetches[4 + pulses :]
    me = lax.axis_index("along")
    group, place = me // GROUP, me % GROUP
    chip, core = place // CORES, place % CORES
    groups = count // GROUP
    mate_place, side_place = chip * CORES + 1 - core, (1 - chip) * CORES + core
    far_place = GROUP - 1 - place
    mate, side = group * GROUP + mate_place, group * GROUP + side_place
    has_below, has_above = group > 0, group < groups - 1
    lowest, second = group == 0, group == 1

    barrier = pltpu.get_barrier_semaphore()

    def greet(other):
        pl.semaphore_signal(barrier, inc=1, device_id={"along": other}, device_id_type=MESH)

    greet(mate)
    greet(side)

    @pl.when(has_below)
    def _():
        greet(me - GROUP)
        greet(side - GROUP)

    @pl.when(has_above)
    def _():
        greet(me + GROUP)
        greet(side + GROUP)

    for fetch in fetches:
        fetch.start()

    def remote(source, landing, send, recv, device):
        return pltpu.make_async_remote_copy(
            src_ref=source, dst_ref=landing, send_sem=send, recv_sem=recv,
            device_id={"along": device}, device_id_type=MESH,
        )

    def to_side(chunk, pulse):
        return remote(
            outbox.at[chunk, pulse], got.at[chunk, place, pulse],
            side_send.at[chunk, pulse], side_recv.at[chunk, pulse], side,
        )

    def to_mate(chunk, pulse):
        mine = got.at[chunk, place, pulse]
        return remote(mine, mine, mate_send.at[chunk, pulse], mate_recv.at[chunk, pulse], mate)

    def pass_on(chunk, pulse):
        theirs = got.at[chunk, side_place, pulse]
        return remote(theirs, theirs, pass_send.at[chunk, pulse], pass_recv.at[chunk, pulse], mate)

    def risen_place(cross):
        return side_place if cross else place

    def rise(cross, pulse):
        return remote(
            got.at[FIRST, risen_place(cross), pulse], below.at[risen_place(cross), pulse],
            rise_send.at[cross, pulse], rise_recv.at[cross, pulse], me + GROUP,
        )

    def share(cross, pulse):
        risen = below.at[risen_place(cross), pulse]
        return remote(risen, risen, share_send.at[cross, pulse], share_recv.at[cross, pulse], mate)

    def to_above(step, pick, chunk):
        return remote(
            outgoing.at[step - 1, pick, chunk], incoming.at[step - 2, pick, chunk],
            up_send.at[step - 2, pick, chunk], up_recv.at[step - 2, pick, chunk], me + GROUP,
        )

    def to_owner(pick, chunk):
        return remote(
            outgoing.at[0, pick, chunk], arrived.at[chip, chunk],
            last_send.at[pick, chunk], last_recv.at[chip, chunk],
            (group + 1) * GROUP + core + CORES * pick,
        )

    def from_below(half, chunk):
        return remote(
            arrived.at[half, chunk], arrived.at[half, chunk],
            last_send.at[half, chunk], last_recv.at[half, chunk], side,
        )

    def across(chunk):
        return remote(
            across_out.at[chunk], across_in.at[chunk], across_send.at[chunk], across_recv.at[chunk], side
        )

    every = tuple(range(CHUNKS))
    first_lanes = lax.broadcasted_iota(jnp.int32, (beams, LANES), 1) < quarter

    def form(pulse, half):
        one = jnp.dot(turned[0], straight[pulse, half], preferred_element_type=jnp.float32)
        two = jnp.dot(turned[1], straight[pulse, half], preferred_element_type=jnp.float32)
        real, imag = one[:, :LANES] - two[:, LANES:], one[:, LANES:] + two[:, :LANES]
        return (
            jnp.where(first_lanes, real, pltpu.roll(imag, quarter, 1)).astype(jnp.bfloat16),
            jnp.where(first_lanes, pltpu.roll(real, quarter, 1), imag).astype(jnp.bfloat16),
        )

    fetch_steering.wait()
    turned[0] = steering[0].T
    turned[1] = steering[1].T
    for pulse in range(pulses):
        if pulse == 0:
            for fetch in small:
                fetch.wait()
        fetch_echoes[pulse].wait()
        compensate(pulse, cells, levels, scalars, echoes, straight)
        for chunk, block in enumerate(form(pulse, 1 - chip)):
            outbox[chunk, pulse] = block
        if pulse == 0:
            pl.semaphore_wait(
                barrier, 2 + 2 * has_below.astype(jnp.int32) + 2 * has_above.astype(jnp.int32)
            )
        to_side(FIRST, pulse).start()
    for pulse in range(pulses):
        for chunk, block in enumerate(form(pulse, chip)):
            got[chunk, place, pulse] = block
        to_mate(FIRST, pulse).start()
        pl.when(lowest & has_above)(rise(0, pulse).start)
    for pulse in range(pulses):
        to_side(LAST, pulse).start()
        to_mate(LAST, pulse).start()

    def reaches(step):
        return group + step < groups

    def forward(chunk):
        for pulse in range(pulses):
            to_side(chunk, pulse).wait_recv()
            pass_on(chunk, pulse).start()
            if chunk == FIRST:
                pl.when(lowest & has_above)(rise(1, pulse).start)

    def collect(chunk):
        for pulse in range(pulses):
            to_mate(chunk, pulse).wait_recv()
            pass_on(chunk, pulse).wait_recv()

    row = lax.broadcasted_iota(jnp.int32, (TILE_X // 8, 8, LANES), 1)
    low_lanes = lax.broadcasted_iota(jnp.int32, (window, LANES), 1) < quarter

    def jitter(step, pick):
        tile = (group + step) * GROUP + core + CORES * pick
        return jnp.clip(anchors[tile] - tile * TILE_X, -JITTER, JITTER) + JITTER

    def beams_of(*chunks):
        def fetch(source, pulse):
            parts = [got[chunk, source, pulse] for chunk in chunks]
            return parts[0] if len(parts) == 1 else jnp.concatenate(parts, 1)

        return fetch

    def beams_below(source, pulse):
        return below[source, pulse]

    def term(step, pick, parts, source, pulse, aligned, guard):
        blocks = GROUP * step + core + CORES * pick - source
        if guard is not None:
            blocks = jnp.clip(blocks, 0, STEPS - 1)
            parts = jnp.where(guard(source), parts, jnp.zeros_like(parts))
        start = TILE_X // SLAB * blocks + spacing // SLAB * (pulses - 1 - pulse)
        slabs = pl.ds(start + aligned, window // SLAB)
        turns = [table[slabs, :, cut].reshape(window, beams) for cut in (slice(0, beams), slice(beams, 2 * beams))]
        return jnp.dot(jnp.concatenate(turns, 0), parts, preferred_element_type=jnp.float32)

    def combine_parts(both):
        second = pltpu.roll(both[window:], quarter, 1)
        return both[:window] + jnp.where(low_lanes, -second, second)

    def settle(value, offset):
        late = jnp.full((window - 8, LANES), offset, jnp.int32) >= 8
        value = jnp.where(late, value[8:], value[:-8])
        value = value.reshape(TILE_X // 8 + 1, 8, LANES)
        ahead = lax.rem(offset, 8)
        value = pltpu.roll(value, lax.rem(8 - ahead, 8), 1)
        value = jnp.where(row < 8 - ahead, value[:-1], value[1:])
        return value.reshape(TILE_X, LANES)

    def project(step, pick, fetch, guard=None, rises=0, sources=range(GROUP)):
        shift = jitter(step, pick)
        aligned, offset = lax.div(shift, SLAB), lax.rem(shift, SLAB)
        both = None
        for source in sources:
            for pulse in range(pulses):
                parts = fetch(source, pulse)
                add = term(step + rises, pick, parts, source, pulse, aligned, guard)
                both = add if both is None else both + add
        return [
            settle(combine_parts(both[:, n : n + LANES]), offset) for n in range(0, both.shape[1], LANES)
        ]

    def beyond(pick):
        return lambda source: source > core + CORES * pick

    def within(pick):
        return lambda source: source <= core + CORES * pick

    def send(step, pick, chunk, value):
        outgoing[step - 1, pick, chunk] = value.astype(jnp.bfloat16)
        pl.when(step > 1)(lambda: to_above(step, pick, chunk).start())
        pl.when(step == 1)(lambda: to_owner(pick, chunk).start())

    def each_pick(active):
        def run(body):
            @pl.when(active)
            def _():
                pl.loop(0, PAIR)(body)

        return run

    def keep(step, pick, chunks, values):
        for chunk, value in zip(chunks, values):
            held[step - 1, pick, chunk] = value

    def add_below(step, sources=range(GROUP)):
        @each_pick(second & reaches(step))
        def _(pick):
            guard = beyond(pick) if step + 1 == REACH else None
            (value,) = project(step, pick, beams_below, guard, 1, sources)
            send(step, pick, FIRST, held[step - 1, pick, FIRST] + value)

    def combine(step, chunk):
        active = group > 1 if chunk == FIRST else has_below

        @each_pick(active & reaches(step))
        def _(pick):
            to_above(step + 1, pick, chunk).wait_recv()
            value = held[step - 1, pick, chunk] + incoming[step - 1, pick, chunk].astype(jnp.float32)
            send(step, pick, chunk, value)

    def own_group(active, rises):
        @each_pick(active)
        def _(turn):
            pick = lax.rem(1 - chip + turn, PAIR)
            values = project(0, pick, beams_of(*every), within(pick))
            if rises:
                values[FIRST] += project(0, pick, beams_below, None, 1)[0]

            @pl.when(turn == 0)
            def _():
                for chunk, value in zip(every, values):
                    across_out[chunk] = value.astype(jnp.bfloat16)
                    across(chunk).start()

            @pl.when(turn > 0)
            def _():
                for chunk, value in zip(every, values):
                    own[chunk] = value

    final_lanes = lax.broadcasted_iota(jnp.int32, (TILE_X, LANES), 1) < quarter

    def finish():
        for chunk in range(CHUNKS):
            across(chunk).wait_recv()
        for half in range(HALVES):
            for chunk in range(CHUNKS):
                mine, theirs = own[chunk], across_in[chunk].astype(jnp.float32)
                final[half, chunk] = jnp.where(chip == half, mine, theirs)

        for chunk in range(CHUNKS):

            @pl.when(group > 1 if chunk == FIRST else has_below)
            def _():
                for half in range(HALVES):
                    from_below(half, chunk).wait_recv()
                    final[half, chunk] += arrived[half, chunk].astype(jnp.float32)

        for half in range(HALVES):
            one, two = final[half, 0], final[half, 1]
            cut = slice(half * LANES, (half + 1) * LANES)
            real = jnp.where(final_lanes, one, pltpu.roll(two, quarter, 1))
            imag = jnp.where(final_lanes, pltpu.roll(one, quarter, 1), two)
            image[0, :, cut] = real.astype(jnp.bfloat16)
            image[1, :, cut] = imag.astype(jnp.bfloat16)

    forward(FIRST)
    fetch_anchors.wait()
    fetch_table.wait()
    collect(FIRST)
    early = REACH - 2
    each_pick(has_below & reaches(early))(
        lambda pick: keep(early, pick, (FIRST,), project(early, pick, beams_of(FIRST)))
    )
    @pl.when(second)
    def _():
        for pulse in range(pulses):
            for cross in range(2):
                rise(cross, pulse).wait_recv()
                share(cross, pulse).start()

    @each_pick(second & reaches(early))
    def _(pick):
        (value,) = project(early, pick, beams_below, None, 1, (place, side_place))
        held[early - 1, pick, FIRST] += value

    @pl.when(second)
    def _():
        for pulse in range(pulses):
            for cross in range(2):
                share(cross, pulse).wait_recv()

    add_below(early, (mate_place, far_place))
    forward(LAST)
    collect(LAST)

    @pl.when(lowest)
    def _():
        @pl.loop(0, (REACH - 1) * PAIR)
        def _(item):
            step, pick = REACH - 1 - item // PAIR, item % PAIR

            @pl.when(reaches(step))
            def _():
                send(step, pick, LAST, project(step, pick, beams_of(LAST))[0])

        @each_pick(reaches(REACH))
        def _(pick):
            send(REACH, pick, LAST, project(REACH, pick, beams_of(LAST), beyond(pick))[0])

    each_pick(has_below & reaches(early))(
        lambda pick: keep(early, pick, (LAST,), project(early, pick, beams_of(LAST)))
    )

    @each_pick(has_below & reaches(REACH))
    def _(pick):
        for chunk, value in zip(every, project(REACH, pick, beams_of(*every), beyond(pick))):
            send(REACH, pick, chunk, value)

    for step in (early, REACH - 1, *range(early - 1, 0, -1)):
        if step != early:
            each_pick(has_below & reaches(step))(
                lambda pick: keep(step, pick, every, project(step, pick, beams_of(*every)))
            )
            add_below(step)
        if step == 1:
            own_group(jnp.logical_not(second), False)
        for chunk in (LAST, FIRST):
            combine(step, chunk)
    own_group(second, True)
    finish()

    for pulse in range(pulses):
        for chunk in every:
            to_side(chunk, pulse).wait_send()
            to_mate(chunk, pulse).wait_send()
            pass_on(chunk, pulse).wait_send()
        for cross in range(2):
            pl.when(lowest & has_above)(rise(cross, pulse).wait_send)
            pl.when(second)(share(cross, pulse).wait_send)
    for chunk in every:
        across(chunk).wait_send()
        active = has_below if chunk == FIRST else group >= 0
        for pick in range(PAIR):
            for step in range(2, REACH + 1):
                pl.when(active & reaches(step))(to_above(step, pick, chunk).wait_send)
            pl.when(active & has_above)(to_owner(pick, chunk).wait_send)


def local(count, echoes, integer_cell_displacement, fractional_level_label, steering, tile_anchor):
    pulses, bins = echoes.shape[1], echoes.shape[4]
    channels, beams = steering.shape[1:]
    spacing = TILE_X // pulses
    first = -JITTER - spacing * (pulses - 1)
    rows = TILE_X * (STEPS - 1) + spacing * (pulses - 1) + 2 * JITTER + TILE_X + SLAB
    table = jnp.asarray(phase_table(beams, pulses, first, rows))
    scalars = jnp.asarray(scalar_table())
    pair = (CHUNKS, pulses)
    dma = pltpu.SemaphoreType.DMA
    narrow = (TILE_X, LANES)
    return pl.pallas_call(
        functools.partial(image_kernel, count),
        out_shape=pltpu.VMEM((2, TILE_X, bins), jnp.bfloat16),
        in_specs=[pl.BlockSpec(memory_space=pltpu.HBM)] * 7,
        out_specs=pl.BlockSpec(memory_space=pltpu.VMEM),
        scratch_shapes=[
            pltpu.SMEM(tile_anchor.shape, jnp.int32),
            pltpu.SMEM(integer_cell_displacement.shape, jnp.int32),
            pltpu.SMEM(fractional_level_label.shape, jnp.int32),
            pltpu.SMEM(scalars.shape, jnp.float32),
            pltpu.VMEM(echoes.shape, echoes.dtype),
            pltpu.VMEM(steering.shape, steering.dtype),
            pltpu.VMEM(table.shape, table.dtype),
            dma((6 + pulses,)),
            pltpu.VMEM((pulses, HALVES, channels, 2 * LANES), jnp.bfloat16),
            pltpu.VMEM((2, beams, channels), jnp.bfloat16),
            pltpu.VMEM((CHUNKS, pulses, beams, LANES), jnp.bfloat16),
            pltpu.VMEM((CHUNKS, GROUP, pulses, beams, LANES), jnp.bfloat16),
            pltpu.VMEM((GROUP, pulses, beams, LANES), jnp.bfloat16),
            pltpu.VMEM((REACH - 1, PAIR, CHUNKS, *narrow), jnp.float32),
            pltpu.VMEM((CHUNKS, *narrow), jnp.float32),
            pltpu.VMEM((HALVES, CHUNKS, *narrow), jnp.float32),
            pltpu.VMEM((REACH, PAIR, CHUNKS, *narrow), jnp.bfloat16),
            pltpu.VMEM((REACH - 1, PAIR, CHUNKS, *narrow), jnp.bfloat16),
            pltpu.VMEM((HALVES, CHUNKS, *narrow), jnp.bfloat16),
            pltpu.VMEM((CHUNKS, *narrow), jnp.bfloat16),
            pltpu.VMEM((CHUNKS, *narrow), jnp.bfloat16),
            dma((2, pulses)), dma((2, pulses)), dma((2, pulses)), dma((2, pulses)),
            dma(pair), dma(pair), dma(pair), dma(pair), dma(pair), dma(pair),
            dma((REACH - 1, PAIR, CHUNKS)), dma((REACH - 1, PAIR, CHUNKS)),
            dma((PAIR, CHUNKS)), dma((HALVES, CHUNKS)), dma((CHUNKS,)), dma((CHUNKS,)),
        ],
        compiler_params=pltpu.CompilerParams(
            collective_id=0, has_side_effects=True, vmem_limit_bytes=66_781_184
        ),
        name="image",
    )(tile_anchor, integer_cell_displacement, fractional_level_label, scalars, echoes, steering, table)


def solution(mesh):
    placed = (
        P(None, ("scene", "along"), None, None, None),
        P(("scene", "along"), None),
        P(("scene", "along"), None),
        P(),
        P("scene"),
    )
    return jax.shard_map(
        functools.partial(local, mesh.shape["along"]),
        mesh=mesh,
        in_specs=placed,
        out_specs=P(None, ("scene", "along"), None),
        check_vma=False,
    )
```

```python
import functools

import jax
import jax.numpy as jnp
import numpy as np
from jax import lax
from jax.experimental import pallas as pl
from jax.experimental.pallas import tpu as pltpu
from jax.sharding import PartitionSpec as P

TILE_X = 256
STEPS = 16
TAPS = 8
SHIFTS = 16
FRACTION_LEVELS = 16
QUAD = 4093
WAVE_FOURTHS = 37
LANES = 128
SLAB = 16
JITTER = TILE_X // 4
GROUP = 4
CORES = 2
PAIR = GROUP // CORES
REACH = STEPS // GROUP
HALVES = 2
CHUNKS = 2
FIRST, LAST = 0, 1
CYCLE = 4 * FRACTION_LEVELS
MESH = pl.DeviceIdType.MESH


def scalar_table():
    shift = np.arange(TAPS)[None] - (TAPS // 2 - 1) - np.arange(FRACTION_LEVELS)[:, None] / FRACTION_LEVELS
    kernel = np.sinc(shift) * (0.54 + 0.46 * np.cos(np.pi * shift / (TAPS // 2)))
    theta = 2 * np.pi * np.arange(CYCLE) / CYCLE
    return np.concatenate([kernel.ravel(), np.cos(theta), np.sin(theta)]).astype(np.float32)


def phase_table(beams, pulses, first, rows):
    offset = np.mod(np.arange(first, first + rows, dtype=np.int64), QUAD)[:, None]
    beam = np.arange(beams, dtype=np.int64)[None]
    units = (offset * offset + beam * beam * offset + beam * offset * offset) % QUAD
    phi = 2 * np.pi * units / QUAD
    gain = (STEPS * pulses * beams) ** -0.5
    table = gain * np.concatenate([np.cos(phi), np.sin(phi)], 1)
    return table.reshape(rows // SLAB, SLAB, 2 * beams).astype(jnp.bfloat16)


def compensate(pulse, cells, levels, scalars, echoes, straight):
    _, _, transmitters, receivers, _ = echoes.shape
    lane = lax.broadcasted_iota(jnp.int32, (8, LANES), 1)
    stack = 2 * receivers // 8
    reach_back = SHIFTS // 2 + TAPS // 2 - 1
    hop = TAPS // 2
    stays = lax.broadcasted_iota(jnp.int32, (2 * receivers, LANES), 1) < LANES - hop

    def tall(value):
        return jnp.concatenate([value] * stack, 0)

    @pl.loop(0, transmitters, unroll=4)
    def _(sender):
        cell, level = cells[pulse, sender], levels[pulse, sender]
        units = lax.rem(WAVE_FOURTHS * (cell * FRACTION_LEVELS + level), CYCLE)
        cosine = scalars[FRACTION_LEVELS * TAPS + units]
        sine = scalars[FRACTION_LEVELS * TAPS + CYCLE + units]
        both = jnp.concatenate([echoes[0, pulse, sender], echoes[1, pulse, sender]], 0)
        both = both.astype(jnp.float32)
        first, second = both[:, :LANES], both[:, LANES:]
        near, far = [None, None], [None, None]
        for tap in range(hop):
            step = cell - reach_back + tap
            turned = [pltpu.roll(part, lax.rem(2 * LANES - step, LANES), 1) for part in (first, second)]
            spot = lane + step
            begun, not_over = spot >= 0, spot < LANES
            wide = tall(spot)
            swapped = (wide < 0) | (wide >= LANES)
            columns = (
                jnp.where(swapped, turned[1], turned[0]), jnp.where(swapped, turned[0], turned[1])
            )
            weight, later = scalars[level * TAPS + tap], scalars[level * TAPS + hop + tap]
            weights = [jnp.where(begun, weight, 0.0), jnp.where(not_over, weight, 0.0)]
            laters = [jnp.where(begun ^ (lane < hop), later, 0.0), jnp.where(not_over, later, 0.0)]
            for c, column in enumerate(columns):
                add, add_far = tall(weights[c]) * column, tall(laters[c]) * column
                near[c] = add if tap == 0 else near[c] + add
                far[c] = add_far if tap == 0 else far[c] + add_far
        ahead = [pltpu.roll(part, LANES - hop, 1) for part in far]
        sums = [
            near[0] + jnp.where(stays, ahead[0], ahead[1]), near[1] + jnp.where(stays, ahead[1], ahead[0])
        ]
        rows = pl.ds(pl.multiple_of(sender * receivers, receivers), receivers)
        for half in range(HALVES):
            a, b = sums[half][:receivers], sums[half][receivers:]
            straight[pulse, half, rows, :LANES] = (cosine * a + sine * b).astype(jnp.bfloat16)
            straight[pulse, half, rows, LANES:] = (cosine * b - sine * a).astype(jnp.bfloat16)


def image_kernel(
    count, far_anchors, far_cells, far_levels, far_scalars, far_echoes, far_steering, far_table, image,
    anchors, cells, levels, scalars, echoes, steering, table, fetched,
    straight, turned, outbox, got, below, held, own, final, outgoing, incoming, arrived, across_out, across_in,
    rise_send, rise_recv, share_send, share_recv, mate_send, mate_recv, side_send, side_recv, pass_send, pass_recv,
    up_send, up_recv, last_send, last_recv, across_send, across_recv,
):
    pulses = echoes.shape[1]
    beams = steering.shape[2]
    spacing = TILE_X // pulses
    window = TILE_X + SLAB
    quarter = LANES // CHUNKS
    pieces = [
        (far_cells, cells), (far_levels, levels), (far_scalars, scalars),
        (far_steering, steering),
        *[(far_echoes.at[:, pulse], echoes.at[:, pulse]) for pulse in range(pulses)],
        (far_anchors, anchors), (far_table, table),
    ]
    fetches = [
        pltpu.make_async_copy(source, landing, fetched.at[number])
        for number, (source, landing) in enumerate(pieces)
    ]
    small, fetch_steering, fetch_echoes = fetches[:3], fetches[3], fetches[4 : 4 + pulses]
    fetch_anchors, fetch_table = fetches[4 + pulses :]
    me = lax.axis_index("along")
    group, place = me // GROUP, me % GROUP
    chip, core = place // CORES, place % CORES
    groups = count // GROUP
    mate_place, side_place = chip * CORES + 1 - core, (1 - chip) * CORES + core
    far_place = GROUP - 1 - place
    mate, side = group * GROUP + mate_place, group * GROUP + side_place
    has_below, has_above = group > 0, group < groups - 1
    lowest, second = group == 0, group == 1

    barrier = pltpu.get_barrier_semaphore()

    def greet(other):
        pl.semaphore_signal(barrier, inc=1, device_id={"along": other}, device_id_type=MESH)

    greet(mate)
    greet(side)

    @pl.when(has_below)
    def _():
        greet(me - GROUP)
        greet(side - GROUP)

    @pl.when(has_above)
    def _():
        greet(me + GROUP)
        greet(side + GROUP)

    for fetch in fetches:
        fetch.start()

    def remote(source, landing, send, recv, device):
        return pltpu.make_async_remote_copy(
            src_ref=source, dst_ref=landing, send_sem=send, recv_sem=recv,
            device_id={"along": device}, device_id_type=MESH,
        )

    def to_side(chunk, pulse):
        return remote(
            outbox.at[chunk, pulse], got.at[chunk, place, pulse],
            side_send.at[chunk, pulse], side_recv.at[chunk, pulse], side,
        )

    def to_mate(chunk, pulse):
        mine = got.at[chunk, place, pulse]
        return remote(mine, mine, mate_send.at[chunk, pulse], mate_recv.at[chunk, pulse], mate)

    def pass_on(chunk, pulse):
        theirs = got.at[chunk, side_place, pulse]
        return remote(theirs, theirs, pass_send.at[chunk, pulse], pass_recv.at[chunk, pulse], mate)

    def risen_place(cross):
        return side_place if cross else place

    def rise(cross, pulse):
        return remote(
            got.at[FIRST, risen_place(cross), pulse], below.at[risen_place(cross), pulse],
            rise_send.at[cross, pulse], rise_recv.at[cross, pulse], me + GROUP,
        )

    def share(cross, pulse):
        risen = below.at[risen_place(cross), pulse]
        return remote(risen, risen, share_send.at[cross, pulse], share_recv.at[cross, pulse], mate)

    def to_above(step, pick, chunk):
        return remote(
            outgoing.at[step - 1, pick, chunk], incoming.at[step - 2, pick, chunk],
            up_send.at[step - 2, pick, chunk], up_recv.at[step - 2, pick, chunk], me + GROUP,
        )

    def to_owner(pick, chunk):
        return remote(
            outgoing.at[0, pick, chunk], arrived.at[chip, chunk],
            last_send.at[pick, chunk], last_recv.at[chip, chunk],
            (group + 1) * GROUP + core + CORES * pick,
        )

    def from_below(half, chunk):
        return remote(
            arrived.at[half, chunk], arrived.at[half, chunk],
            last_send.at[half, chunk], last_recv.at[half, chunk], side,
        )

    def across(chunk):
        return remote(
            across_out.at[chunk], across_in.at[chunk], across_send.at[chunk], across_recv.at[chunk], side
        )

    every = tuple(range(CHUNKS))
    first_lanes = lax.broadcasted_iota(jnp.int32, (beams, LANES), 1) < quarter

    def form(pulse, half):
        one = jnp.dot(turned[0], straight[pulse, half], preferred_element_type=jnp.float32)
        two = jnp.dot(turned[1], straight[pulse, half], preferred_element_type=jnp.float32)
        real, imag = one[:, :LANES] - two[:, LANES:], one[:, LANES:] + two[:, :LANES]
        return (
            jnp.where(first_lanes, real, pltpu.roll(imag, quarter, 1)).astype(jnp.bfloat16),
            jnp.where(first_lanes, pltpu.roll(real, quarter, 1), imag).astype(jnp.bfloat16),
        )

    fetch_steering.wait()
    turned[0] = steering[0].T
    turned[1] = steering[1].T
    for pulse in range(pulses):
        if pulse == 0:
            for fetch in small:
                fetch.wait()
        fetch_echoes[pulse].wait()
        compensate(pulse, cells, levels, scalars, echoes, straight)
        for chunk, block in enumerate(form(pulse, 1 - chip)):
            outbox[chunk, pulse] = block
        if pulse == 0:
            pl.semaphore_wait(
                barrier, 2 + 2 * has_below.astype(jnp.int32) + 2 * has_above.astype(jnp.int32)
            )
        to_side(FIRST, pulse).start()
    for pulse in range(pulses):
        for chunk, block in enumerate(form(pulse, chip)):
            got[chunk, place, pulse] = block
        to_mate(FIRST, pulse).start()
        pl.when(lowest & has_above)(rise(0, pulse).start)
    for pulse in range(pulses):
        to_side(FIRST, pulse).wait_send()
    for pulse in range(pulses):
        to_side(LAST, pulse).start()
        to_mate(LAST, pulse).start()

    def reaches(step):
        return group + step < groups

    def forward(chunk):
        for pulse in range(pulses):
            to_side(chunk, pulse).wait_recv()
            pass_on(chunk, pulse).start()
            if chunk == FIRST:
                pl.when(lowest & has_above)(rise(1, pulse).start)

    def collect(chunk):
        for pulse in range(pulses):
            to_mate(chunk, pulse).wait_recv()
            pass_on(chunk, pulse).wait_recv()

    row = lax.broadcasted_iota(jnp.int32, (TILE_X // 8, 8, LANES), 1)
    low_lanes = lax.broadcasted_iota(jnp.int32, (window, LANES), 1) < quarter

    def jitter(step, pick):
        tile = (group + step) * GROUP + core + CORES * pick
        return jnp.clip(anchors[tile] - tile * TILE_X, -JITTER, JITTER) + JITTER

    def beams_of(*chunks):
        def fetch(source, pulse):
            parts = [got[chunk, source, pulse] for chunk in chunks]
            return parts[0] if len(parts) == 1 else jnp.concatenate(parts, 1)

        return fetch

    def beams_below(source, pulse):
        return below[source, pulse]

    def term(step, pick, parts, source, pulse, aligned, guard):
        blocks = GROUP * step + core + CORES * pick - source
        if guard is not None:
            blocks = jnp.clip(blocks, 0, STEPS - 1)
            parts = jnp.where(guard(source), parts, jnp.zeros_like(parts))
        start = TILE_X // SLAB * blocks + spacing // SLAB * (pulses - 1 - pulse)
        slabs = pl.ds(start + aligned, window // SLAB)
        turns = [table[slabs, :, cut].reshape(window, beams) for cut in (slice(0, beams), slice(beams, 2 * beams))]
        return jnp.dot(jnp.concatenate(turns, 0), parts, preferred_element_type=jnp.float32)

    def combine_parts(both):
        second = pltpu.roll(both[window:], quarter, 1)
        return both[:window] + jnp.where(low_lanes, -second, second)

    def settle(value, offset):
        late = jnp.full((window - 8, LANES), offset, jnp.int32) >= 8
        value = jnp.where(late, value[8:], value[:-8])
        value = value.reshape(TILE_X // 8 + 1, 8, LANES)
        ahead = lax.rem(offset, 8)
        value = pltpu.roll(value, lax.rem(8 - ahead, 8), 1)
        value = jnp.where(row < 8 - ahead, value[:-1], value[1:])
        return value.reshape(TILE_X, LANES)

    def project(step, pick, fetch, guard=None, rises=0, sources=range(GROUP)):
        shift = jitter(step, pick)
        aligned, offset = lax.div(shift, SLAB), lax.rem(shift, SLAB)
        both = None
        for source in sources:
            for pulse in range(pulses):
                parts = fetch(source, pulse)
                add = term(step + rises, pick, parts, source, pulse, aligned, guard)
                both = add if both is None else both + add
        return [
            settle(combine_parts(both[:, n : n + LANES]), offset) for n in range(0, both.shape[1], LANES)
        ]

    def beyond(pick):
        return lambda source: source > core + CORES * pick

    def within(pick):
        return lambda source: source <= core + CORES * pick

    def send(step, pick, chunk, value):
        outgoing[step - 1, pick, chunk] = value.astype(jnp.bfloat16)
        pl.when(step > 1)(lambda: to_above(step, pick, chunk).start())
        pl.when(step == 1)(lambda: to_owner(pick, chunk).start())

    def each_pick(active):
        def run(body):
            @pl.when(active)
            def _():
                pl.loop(0, PAIR)(body)

        return run

    def keep(step, pick, chunks, values):
        for chunk, value in zip(chunks, values):
            held[step - 1, pick, chunk] = value

    def add_below(step, sources=range(GROUP)):
        @each_pick(second & reaches(step))
        def _(pick):
            guard = beyond(pick) if step + 1 == REACH else None
            (value,) = project(step, pick, beams_below, guard, 1, sources)
            send(step, pick, FIRST, held[step - 1, pick, FIRST] + value)

    def combine(step, chunk):
        active = group > 1 if chunk == FIRST else has_below

        @each_pick(active & reaches(step))
        def _(pick):
            to_above(step + 1, pick, chunk).wait_recv()
            value = held[step - 1, pick, chunk] + incoming[step - 1, pick, chunk].astype(jnp.float32)
            send(step, pick, chunk, value)

    def own_group(active, rises):
        @each_pick(active)
        def _(turn):
            pick = lax.rem(1 - chip + turn, PAIR)
            values = project(0, pick, beams_of(*every), within(pick))
            if rises:
                values[FIRST] += project(0, pick, beams_below, None, 1)[0]

            @pl.when(turn == 0)
            def _():
                for chunk, value in zip(every, values):
                    across_out[chunk] = value.astype(jnp.bfloat16)
                    across(chunk).start()

            @pl.when(turn > 0)
            def _():
                for chunk, value in zip(every, values):
                    own[chunk] = value

    final_lanes = lax.broadcasted_iota(jnp.int32, (TILE_X, LANES), 1) < quarter

    def finish():
        for chunk in range(CHUNKS):
            across(chunk).wait_recv()
        for half in range(HALVES):
            for chunk in range(CHUNKS):
                mine, theirs = own[chunk], across_in[chunk].astype(jnp.float32)
                final[half, chunk] = jnp.where(chip == half, mine, theirs)

        for chunk in range(CHUNKS):

            @pl.when(group > 1 if chunk == FIRST else has_below)
            def _():
                for half in range(HALVES):
                    from_below(half, chunk).wait_recv()
                    final[half, chunk] += arrived[half, chunk].astype(jnp.float32)

        for half in range(HALVES):
            one, two = final[half, 0], final[half, 1]
            cut = slice(half * LANES, (half + 1) * LANES)
            real = jnp.where(final_lanes, one, pltpu.roll(two, quarter, 1))
            imag = jnp.where(final_lanes, pltpu.roll(one, quarter, 1), two)
            image[0, :, cut] = real.astype(jnp.bfloat16)
            image[1, :, cut] = imag.astype(jnp.bfloat16)

    forward(FIRST)
    fetch_anchors.wait()
    fetch_table.wait()
    collect(FIRST)
    early = REACH - 2
    each_pick(has_below & reaches(early))(
        lambda pick: keep(early, pick, (FIRST,), project(early, pick, beams_of(FIRST)))
    )
    @pl.when(second)
    def _():
        for pulse in range(pulses):
            for cross in range(2):
                rise(cross, pulse).wait_recv()
                share(cross, pulse).start()

    @each_pick(second & reaches(early))
    def _(pick):
        (value,) = project(early, pick, beams_below, None, 1, (place, side_place))
        held[early - 1, pick, FIRST] += value

    forward(LAST)

    @pl.when(second)
    def _():
        for pulse in range(pulses):
            for cross in range(2):
                share(cross, pulse).wait_recv()

    add_below(early, (mate_place, far_place))
    collect(LAST)

    @pl.when(lowest)
    def _():
        @pl.loop(0, (REACH - 1) * PAIR)
        def _(item):
            step, pick = REACH - 1 - item // PAIR, item % PAIR

            @pl.when(reaches(step))
            def _():
                send(step, pick, LAST, project(step, pick, beams_of(LAST))[0])

        @each_pick(reaches(REACH))
        def _(pick):
            send(REACH, pick, LAST, project(REACH, pick, beams_of(LAST), beyond(pick))[0])

    each_pick(has_below & reaches(early))(
        lambda pick: keep(early, pick, (LAST,), project(early, pick, beams_of(LAST)))
    )

    @each_pick(has_below & reaches(REACH))
    def _(pick):
        for chunk, value in zip(every, project(REACH, pick, beams_of(*every), beyond(pick))):
            send(REACH, pick, chunk, value)

    for step in (early, REACH - 1, *range(early - 1, 0, -1)):
        if step != early:
            each_pick(has_below & reaches(step))(
                lambda pick: keep(step, pick, every, project(step, pick, beams_of(*every)))
            )
            add_below(step)
        if step == 1:
            own_group(jnp.logical_not(second), False)
        for chunk in (LAST, FIRST):
            combine(step, chunk)
    own_group(second, True)
    finish()

    for pulse in range(pulses):
        for chunk in every:
            if chunk != FIRST:
                to_side(chunk, pulse).wait_send()
            to_mate(chunk, pulse).wait_send()
            pass_on(chunk, pulse).wait_send()
        for cross in range(2):
            pl.when(lowest & has_above)(rise(cross, pulse).wait_send)
            pl.when(second)(share(cross, pulse).wait_send)
    for chunk in every:
        across(chunk).wait_send()
        active = has_below if chunk == FIRST else group >= 0
        for pick in range(PAIR):
            for step in range(2, REACH + 1):
                pl.when(active & reaches(step))(to_above(step, pick, chunk).wait_send)
            pl.when(active & has_above)(to_owner(pick, chunk).wait_send)


def local(count, echoes, integer_cell_displacement, fractional_level_label, steering, tile_anchor):
    pulses, bins = echoes.shape[1], echoes.shape[4]
    channels, beams = steering.shape[1:]
    spacing = TILE_X // pulses
    first = -JITTER - spacing * (pulses - 1)
    rows = TILE_X * (STEPS - 1) + spacing * (pulses - 1) + 2 * JITTER + TILE_X + SLAB
    table = jnp.asarray(phase_table(beams, pulses, first, rows))
    scalars = jnp.asarray(scalar_table())
    pair = (CHUNKS, pulses)
    dma = pltpu.SemaphoreType.DMA
    narrow = (TILE_X, LANES)
    return pl.pallas_call(
        functools.partial(image_kernel, count),
        out_shape=pltpu.VMEM((2, TILE_X, bins), jnp.bfloat16),
        in_specs=[pl.BlockSpec(memory_space=pltpu.HBM)] * 7,
        out_specs=pl.BlockSpec(memory_space=pltpu.VMEM),
        scratch_shapes=[
            pltpu.SMEM(tile_anchor.shape, jnp.int32),
            pltpu.SMEM(integer_cell_displacement.shape, jnp.int32),
            pltpu.SMEM(fractional_level_label.shape, jnp.int32),
            pltpu.SMEM(scalars.shape, jnp.float32),
            pltpu.VMEM(echoes.shape, echoes.dtype),
            pltpu.VMEM(steering.shape, steering.dtype),
            pltpu.VMEM(table.shape, table.dtype),
            dma((6 + pulses,)),
            pltpu.VMEM((pulses, HALVES, channels, 2 * LANES), jnp.bfloat16),
            pltpu.VMEM((2, beams, channels), jnp.bfloat16),
            pltpu.VMEM((CHUNKS, pulses, beams, LANES), jnp.bfloat16),
            pltpu.VMEM((CHUNKS, GROUP, pulses, beams, LANES), jnp.bfloat16),
            pltpu.VMEM((GROUP, pulses, beams, LANES), jnp.bfloat16),
            pltpu.VMEM((REACH - 1, PAIR, CHUNKS, *narrow), jnp.float32),
            pltpu.VMEM((CHUNKS, *narrow), jnp.float32),
            pltpu.VMEM((HALVES, CHUNKS, *narrow), jnp.float32),
            pltpu.VMEM((REACH, PAIR, CHUNKS, *narrow), jnp.bfloat16),
            pltpu.VMEM((REACH - 1, PAIR, CHUNKS, *narrow), jnp.bfloat16),
            pltpu.VMEM((HALVES, CHUNKS, *narrow), jnp.bfloat16),
            pltpu.VMEM((CHUNKS, *narrow), jnp.bfloat16),
            pltpu.VMEM((CHUNKS, *narrow), jnp.bfloat16),
            dma((2, pulses)), dma((2, pulses)), dma((2, pulses)), dma((2, pulses)),
            dma(pair), dma(pair), dma(pair), dma(pair), dma(pair), dma(pair),
            dma((REACH - 1, PAIR, CHUNKS)), dma((REACH - 1, PAIR, CHUNKS)),
            dma((PAIR, CHUNKS)), dma((HALVES, CHUNKS)), dma((CHUNKS,)), dma((CHUNKS,)),
        ],
        compiler_params=pltpu.CompilerParams(
            collective_id=0, has_side_effects=True, vmem_limit_bytes=66_781_184
        ),
        name="image",
    )(tile_anchor, integer_cell_displacement, fractional_level_label, scalars, echoes, steering, table)


def solution(mesh):
    placed = (
        P(None, ("scene", "along"), None, None, None),
        P(("scene", "along"), None),
        P(("scene", "along"), None),
        P(),
        P("scene"),
    )
    return jax.shard_map(
        functools.partial(local, mesh.shape["along"]),
        mesh=mesh,
        in_specs=placed,
        out_specs=P(None, ("scene", "along"), None),
        check_vma=False,
    )
```

```python
import functools

import jax
import jax.numpy as jnp
import numpy as np
from jax import lax
from jax.experimental import pallas as pl
from jax.experimental.pallas import tpu as pltpu
from jax.sharding import PartitionSpec as P

TILE_X = 256
STEPS = 16
TAPS = 8
SHIFTS = 16
FRACTION_LEVELS = 16
QUAD = 4093
WAVE_FOURTHS = 37
LANES = 128
SLAB = 16
JITTER = TILE_X // 4
GROUP = 4
CORES = 2
PAIR = GROUP // CORES
REACH = STEPS // GROUP
HALVES = 2
CHUNKS = 2
FIRST, LAST = 0, 1
CYCLE = 4 * FRACTION_LEVELS
MESH = pl.DeviceIdType.MESH


def scalar_table():
    shift = np.arange(TAPS)[None] - (TAPS // 2 - 1) - np.arange(FRACTION_LEVELS)[:, None] / FRACTION_LEVELS
    kernel = np.sinc(shift) * (0.54 + 0.46 * np.cos(np.pi * shift / (TAPS // 2)))
    theta = 2 * np.pi * np.arange(CYCLE) / CYCLE
    return np.concatenate([kernel.ravel(), np.cos(theta), np.sin(theta)]).astype(np.float32)


def phase_table(beams, pulses, first, rows):
    offset = np.mod(np.arange(first, first + rows, dtype=np.int64), QUAD)[:, None]
    beam = np.arange(beams, dtype=np.int64)[None]
    units = (offset * offset + beam * beam * offset + beam * offset * offset) % QUAD
    phi = 2 * np.pi * units / QUAD
    gain = (STEPS * pulses * beams) ** -0.5
    table = gain * np.concatenate([np.cos(phi), np.sin(phi)], 1)
    return table.reshape(rows // SLAB, SLAB, 2 * beams).astype(jnp.bfloat16)


def compensate(pulse, cells, levels, scalars, echoes, straight):
    _, _, transmitters, receivers, _ = echoes.shape
    lane = lax.broadcasted_iota(jnp.int32, (8, LANES), 1)
    stack = 2 * receivers // 8
    reach_back = SHIFTS // 2 + TAPS // 2 - 1
    hop = TAPS // 2
    stays = lax.broadcasted_iota(jnp.int32, (2 * receivers, LANES), 1) < LANES - hop

    def tall(value):
        return jnp.concatenate([value] * stack, 0)

    @pl.loop(0, transmitters, unroll=4)
    def _(sender):
        cell, level = cells[pulse, sender], levels[pulse, sender]
        units = lax.rem(WAVE_FOURTHS * (cell * FRACTION_LEVELS + level), CYCLE)
        cosine = scalars[FRACTION_LEVELS * TAPS + units]
        sine = scalars[FRACTION_LEVELS * TAPS + CYCLE + units]
        both = jnp.concatenate([echoes[0, pulse, sender], echoes[1, pulse, sender]], 0)
        both = both.astype(jnp.float32)
        first, second = both[:, :LANES], both[:, LANES:]
        near, far = [None, None], [None, None]
        for tap in range(hop):
            step = cell - reach_back + tap
            turned = [pltpu.roll(part, lax.rem(2 * LANES - step, LANES), 1) for part in (first, second)]
            spot = lane + step
            begun, not_over = spot >= 0, spot < LANES
            wide = tall(spot)
            swapped = (wide < 0) | (wide >= LANES)
            columns = (
                jnp.where(swapped, turned[1], turned[0]), jnp.where(swapped, turned[0], turned[1])
            )
            weight, later = scalars[level * TAPS + tap], scalars[level * TAPS + hop + tap]
            weights = [jnp.where(begun, weight, 0.0), jnp.where(not_over, weight, 0.0)]
            laters = [jnp.where(begun ^ (lane < hop), later, 0.0), jnp.where(not_over, later, 0.0)]
            for c, column in enumerate(columns):
                add, add_far = tall(weights[c]) * column, tall(laters[c]) * column
                near[c] = add if tap == 0 else near[c] + add
                far[c] = add_far if tap == 0 else far[c] + add_far
        ahead = [pltpu.roll(part, LANES - hop, 1) for part in far]
        sums = [
            near[0] + jnp.where(stays, ahead[0], ahead[1]), near[1] + jnp.where(stays, ahead[1], ahead[0])
        ]
        rows = pl.ds(pl.multiple_of(sender * receivers, receivers), receivers)
        for half in range(HALVES):
            a, b = sums[half][:receivers], sums[half][receivers:]
            straight[pulse, half, rows, :LANES] = (cosine * a + sine * b).astype(jnp.bfloat16)
            straight[pulse, half, rows, LANES:] = (cosine * b - sine * a).astype(jnp.bfloat16)


def image_kernel(
    count, far_anchors, far_cells, far_levels, far_scalars, far_echoes, far_steering, far_table, image,
    anchors, cells, levels, scalars, echoes, steering, table, fetched,
    straight, turned, outbox, got, below, held, own, final, outgoing, incoming, arrived, across_out, across_in,
    rise_send, rise_recv, share_send, share_recv, mate_send, mate_recv, side_send, side_recv, pass_send, pass_recv,
    up_send, up_recv, last_send, last_recv, across_send, across_recv,
):
    pulses = echoes.shape[1]
    beams = steering.shape[2]
    spacing = TILE_X // pulses
    window = TILE_X + SLAB
    quarter = LANES // CHUNKS
    pieces = [
        (far_cells, cells), (far_levels, levels), (far_scalars, scalars),
        (far_steering, steering),
        *[(far_echoes.at[:, pulse], echoes.at[:, pulse]) for pulse in range(pulses)],
        (far_anchors, anchors), (far_table, table),
    ]
    fetches = [
        pltpu.make_async_copy(source, landing, fetched.at[number])
        for number, (source, landing) in enumerate(pieces)
    ]
    small, fetch_steering, fetch_echoes = fetches[:3], fetches[3], fetches[4 : 4 + pulses]
    fetch_anchors, fetch_table = fetches[4 + pulses :]
    me = lax.axis_index("along")
    group, place = me // GROUP, me % GROUP
    chip, core = place // CORES, place % CORES
    groups = count // GROUP
    mate_place, side_place = chip * CORES + 1 - core, (1 - chip) * CORES + core
    far_place = GROUP - 1 - place
    mate, side = group * GROUP + mate_place, group * GROUP + side_place
    has_below, has_above = group > 0, group < groups - 1
    lowest, second = group == 0, group == 1

    barrier = pltpu.get_barrier_semaphore()

    def greet(other):
        pl.semaphore_signal(barrier, inc=1, device_id={"along": other}, device_id_type=MESH)

    greet(mate)
    greet(side)

    @pl.when(has_below)
    def _():
        greet(me - GROUP)
        greet(side - GROUP)

    @pl.when(has_above)
    def _():
        greet(me + GROUP)
        greet(side + GROUP)

    for fetch in fetches:
        fetch.start()

    def remote(source, landing, send, recv, device):
        return pltpu.make_async_remote_copy(
            src_ref=source, dst_ref=landing, send_sem=send, recv_sem=recv,
            device_id={"along": device}, device_id_type=MESH,
        )

    def to_side(chunk, pulse):
        return remote(
            outbox.at[chunk, pulse], got.at[chunk, place, pulse],
            side_send.at[chunk, pulse], side_recv.at[chunk, pulse], side,
        )

    def to_mate(chunk, pulse):
        mine = got.at[chunk, place, pulse]
        return remote(mine, mine, mate_send.at[chunk, pulse], mate_recv.at[chunk, pulse], mate)

    def pass_on(chunk, pulse):
        theirs = got.at[chunk, side_place, pulse]
        return remote(theirs, theirs, pass_send.at[chunk, pulse], pass_recv.at[chunk, pulse], mate)

    def risen_place(cross):
        return side_place if cross else place

    def rise(cross, pulse):
        return remote(
            got.at[FIRST, risen_place(cross), pulse], below.at[risen_place(cross), pulse],
            rise_send.at[cross, pulse], rise_recv.at[cross, pulse], me + GROUP,
        )

    def share(cross, pulse):
        risen = below.at[risen_place(cross), pulse]
        return remote(risen, risen, share_send.at[cross, pulse], share_recv.at[cross, pulse], mate)

    def to_above(step, pick, chunk):
        return remote(
            outgoing.at[step - 1, pick, chunk], incoming.at[step - 2, pick, chunk],
            up_send.at[step - 2, pick, chunk], up_recv.at[step - 2, pick, chunk], me + GROUP,
        )

    def to_owner(pick, chunk):
        return remote(
            outgoing.at[0, pick, chunk], arrived.at[chip, chunk],
            last_send.at[pick, chunk], last_recv.at[chip, chunk],
            (group + 1) * GROUP + core + CORES * pick,
        )

    def from_below(half, chunk):
        return remote(
            arrived.at[half, chunk], arrived.at[half, chunk],
            last_send.at[half, chunk], last_recv.at[half, chunk], side,
        )

    def across(chunk):
        return remote(
            across_out.at[chunk], across_in.at[chunk], across_send.at[chunk], across_recv.at[chunk], side
        )

    every = tuple(range(CHUNKS))
    first_lanes = lax.broadcasted_iota(jnp.int32, (beams, LANES), 1) < quarter

    def form(pulse, half):
        one = jnp.dot(turned[0], straight[pulse, half], preferred_element_type=jnp.float32)
        two = jnp.dot(turned[1], straight[pulse, half], preferred_element_type=jnp.float32)
        real, imag = one[:, :LANES] - two[:, LANES:], one[:, LANES:] + two[:, :LANES]
        return (
            jnp.where(first_lanes, real, pltpu.roll(imag, quarter, 1)).astype(jnp.bfloat16),
            jnp.where(first_lanes, pltpu.roll(real, quarter, 1), imag).astype(jnp.bfloat16),
        )

    fetch_steering.wait()
    turned[0] = steering[0].T
    turned[1] = steering[1].T
    for pulse in range(pulses):
        if pulse == 0:
            for fetch in small:
                fetch.wait()
        fetch_echoes[pulse].wait()
        compensate(pulse, cells, levels, scalars, echoes, straight)
        for chunk, block in enumerate(form(pulse, 1 - chip)):
            outbox[chunk, pulse] = block
        if pulse == 0:
            pl.semaphore_wait(
                barrier, 2 + 2 * has_below.astype(jnp.int32) + 2 * has_above.astype(jnp.int32)
            )
        to_side(FIRST, pulse).start()
    for pulse in range(pulses):
        for chunk, block in enumerate(form(pulse, chip)):
            got[chunk, place, pulse] = block
        to_mate(FIRST, pulse).start()
        pl.when(lowest & has_above)(rise(0, pulse).start)
    for pulse in range(pulses):
        to_side(FIRST, pulse).wait_send()
    for pulse in range(pulses):
        to_side(LAST, pulse).start()
        to_mate(LAST, pulse).start()

    def reaches(step):
        return group + step < groups

    def forward(chunk):
        for pulse in range(pulses):
            to_side(chunk, pulse).wait_recv()
            pass_on(chunk, pulse).start()
            if chunk == FIRST:
                pl.when(lowest & has_above)(rise(1, pulse).start)

    def collect(chunk):
        for pulse in range(pulses):
            to_mate(chunk, pulse).wait_recv()
            pass_on(chunk, pulse).wait_recv()

    row = lax.broadcasted_iota(jnp.int32, (TILE_X // 8, 8, LANES), 1)
    low_lanes = lax.broadcasted_iota(jnp.int32, (window, LANES), 1) < quarter

    def jitter(step, pick):
        tile = (group + step) * GROUP + core + CORES * pick
        return jnp.clip(anchors[tile] - tile * TILE_X, -JITTER, JITTER) + JITTER

    def beams_of(*chunks):
        def fetch(source, pulse):
            parts = [got[chunk, source, pulse] for chunk in chunks]
            return parts[0] if len(parts) == 1 else jnp.concatenate(parts, 1)

        return fetch

    def beams_below(source, pulse):
        return below[source, pulse]

    def term(step, pick, parts, source, pulse, aligned, guard):
        blocks = GROUP * step + core + CORES * pick - source
        if guard is not None:
            blocks = jnp.clip(blocks, 0, STEPS - 1)
            parts = jnp.where(guard(source), parts, jnp.zeros_like(parts))
        start = TILE_X // SLAB * blocks + spacing // SLAB * (pulses - 1 - pulse)
        slabs = pl.ds(start + aligned, window // SLAB)
        turns = [table[slabs, :, cut].reshape(window, beams) for cut in (slice(0, beams), slice(beams, 2 * beams))]
        return jnp.dot(jnp.concatenate(turns, 0), parts, preferred_element_type=jnp.float32)

    def combine_parts(both):
        second = pltpu.roll(both[window:], quarter, 1)
        return both[:window] + jnp.where(low_lanes, -second, second)

    def settle(value, offset):
        late = jnp.full((window - 8, LANES), offset, jnp.int32) >= 8
        value = jnp.where(late, value[8:], value[:-8])
        value = value.reshape(TILE_X // 8 + 1, 8, LANES)
        ahead = lax.rem(offset, 8)
        value = pltpu.roll(value, lax.rem(8 - ahead, 8), 1)
        value = jnp.where(row < 8 - ahead, value[:-1], value[1:])
        return value.reshape(TILE_X, LANES)

    def project(step, pick, fetch, guard=None, rises=0, sources=range(GROUP)):
        shift = jitter(step, pick)
        aligned, offset = lax.div(shift, SLAB), lax.rem(shift, SLAB)
        both = None
        for source in sources:
            for pulse in range(pulses):
                parts = fetch(source, pulse)
                add = term(step + rises, pick, parts, source, pulse, aligned, guard)
                both = add if both is None else both + add
        return [
            settle(combine_parts(both[:, n : n + LANES]), offset) for n in range(0, both.shape[1], LANES)
        ]

    def beyond(pick):
        return lambda source: source > core + CORES * pick

    def within(pick):
        return lambda source: source <= core + CORES * pick

    def send(step, pick, chunk, value):
        outgoing[step - 1, pick, chunk] = value.astype(jnp.bfloat16)
        pl.when(step > 1)(lambda: to_above(step, pick, chunk).start())
        pl.when(step == 1)(lambda: to_owner(pick, chunk).start())

    def each_pick(active):
        def run(body):
            @pl.when(active)
            def _():
                pl.loop(0, PAIR)(body)

        return run

    def keep(step, pick, chunks, values):
        for chunk, value in zip(chunks, values):
            held[step - 1, pick, chunk] = value

    def add_below(step, sources=range(GROUP)):
        @each_pick(second & reaches(step))
        def _(pick):
            guard = beyond(pick) if step + 1 == REACH else None
            (value,) = project(step, pick, beams_below, guard, 1, sources)
            send(step, pick, FIRST, held[step - 1, pick, FIRST] + value)

    def combine(step, chunk):
        active = group > 1 if chunk == FIRST else has_below

        @each_pick(active & reaches(step))
        def _(pick):
            to_above(step + 1, pick, chunk).wait_recv()
            value = held[step - 1, pick, chunk] + incoming[step - 1, pick, chunk].astype(jnp.float32)
            send(step, pick, chunk, value)

    def own_group(active, rises):
        @each_pick(active)
        def _(turn):
            pick = lax.rem(1 - chip + turn, PAIR)
            values = project(0, pick, beams_of(*every), within(pick))
            if rises:
                values[FIRST] += project(0, pick, beams_below, None, 1)[0]

            @pl.when(turn == 0)
            def _():
                for chunk, value in zip(every, values):
                    across_out[chunk] = value.astype(jnp.bfloat16)
                    across(chunk).start()

            @pl.when(turn > 0)
            def _():
                for chunk, value in zip(every, values):
                    own[chunk] = value

    final_lanes = lax.broadcasted_iota(jnp.int32, (TILE_X, LANES), 1) < quarter

    def finish():
        for chunk in range(CHUNKS):
            across(chunk).wait_recv()
        for half in range(HALVES):
            for chunk in range(CHUNKS):
                mine, theirs = own[chunk], across_in[chunk].astype(jnp.float32)
                final[half, chunk] = jnp.where(chip == half, mine, theirs)

        for chunk in range(CHUNKS):

            @pl.when(group > 1 if chunk == FIRST else has_below)
            def _():
                for half in range(HALVES):
                    from_below(half, chunk).wait_recv()
                    final[half, chunk] += arrived[half, chunk].astype(jnp.float32)

        for half in range(HALVES):
            one, two = final[half, 0], final[half, 1]
            cut = slice(half * LANES, (half + 1) * LANES)
            real = jnp.where(final_lanes, one, pltpu.roll(two, quarter, 1))
            imag = jnp.where(final_lanes, pltpu.roll(one, quarter, 1), two)
            image[0, :, cut] = real.astype(jnp.bfloat16)
            image[1, :, cut] = imag.astype(jnp.bfloat16)

    forward(FIRST)
    fetch_anchors.wait()
    fetch_table.wait()
    collect(FIRST)
    early = REACH - 2
    each_pick(has_below & reaches(early))(
        lambda pick: keep(early, pick, (FIRST,), project(early, pick, beams_of(FIRST)))
    )
    @pl.when(second)
    def _():
        for pulse in range(pulses):
            for cross in range(2):
                rise(cross, pulse).wait_recv()
                share(cross, pulse).start()

    @each_pick(second & reaches(early))
    def _(pick):
        (value,) = project(early, pick, beams_below, None, 1, (place, side_place))
        held[early - 1, pick, FIRST] += value

    forward(LAST)

    @each_pick(lowest & reaches(REACH - 1))
    def _(pick):
        near = project(REACH - 1, pick, beams_of(LAST), sources=(place, side_place))
        keep(REACH - 1, pick, (LAST,), near)

    @pl.when(second)
    def _():
        for pulse in range(pulses):
            for cross in range(2):
                share(cross, pulse).wait_recv()

    add_below(early, (mate_place, far_place))
    collect(LAST)

    @pl.when(lowest)
    def _():
        @each_pick(reaches(REACH - 1))
        def _(pick):
            (value,) = project(REACH - 1, pick, beams_of(LAST), sources=(mate_place, far_place))
            send(REACH - 1, pick, LAST, held[REACH - 2, pick, LAST] + value)

        @pl.loop(0, (REACH - 2) * PAIR)
        def _(item):
            step, pick = REACH - 2 - item // PAIR, item % PAIR

            @pl.when(reaches(step))
            def _():
                send(step, pick, LAST, project(step, pick, beams_of(LAST))[0])

        @each_pick(reaches(REACH))
        def _(pick):
            send(REACH, pick, LAST, project(REACH, pick, beams_of(LAST), beyond(pick))[0])

    each_pick(has_below & reaches(early))(
        lambda pick: keep(early, pick, (LAST,), project(early, pick, beams_of(LAST)))
    )

    @each_pick(has_below & reaches(REACH))
    def _(pick):
        for chunk, value in zip(every, project(REACH, pick, beams_of(*every), beyond(pick))):
            send(REACH, pick, chunk, value)

    for step in (early, REACH - 1, *range(early - 1, 0, -1)):
        if step != early:
            each_pick(has_below & reaches(step))(
                lambda pick: keep(step, pick, every, project(step, pick, beams_of(*every)))
            )
            add_below(step)
        if step == 1:
            own_group(jnp.logical_not(second), False)
        for chunk in (LAST, FIRST):
            combine(step, chunk)
    own_group(second, True)
    finish()

    for pulse in range(pulses):
        for chunk in every:
            if chunk != FIRST:
                to_side(chunk, pulse).wait_send()
            to_mate(chunk, pulse).wait_send()
            pass_on(chunk, pulse).wait_send()
        for cross in range(2):
            pl.when(lowest & has_above)(rise(cross, pulse).wait_send)
            pl.when(second)(share(cross, pulse).wait_send)
    for chunk in every:
        across(chunk).wait_send()
        active = has_below if chunk == FIRST else group >= 0
        for pick in range(PAIR):
            for step in range(2, REACH + 1):
                pl.when(active & reaches(step))(to_above(step, pick, chunk).wait_send)
            pl.when(active & has_above)(to_owner(pick, chunk).wait_send)


def local(count, echoes, integer_cell_displacement, fractional_level_label, steering, tile_anchor):
    pulses, bins = echoes.shape[1], echoes.shape[4]
    channels, beams = steering.shape[1:]
    spacing = TILE_X // pulses
    first = -JITTER - spacing * (pulses - 1)
    rows = TILE_X * (STEPS - 1) + spacing * (pulses - 1) + 2 * JITTER + TILE_X + SLAB
    table = jnp.asarray(phase_table(beams, pulses, first, rows))
    scalars = jnp.asarray(scalar_table())
    pair = (CHUNKS, pulses)
    dma = pltpu.SemaphoreType.DMA
    narrow = (TILE_X, LANES)
    return pl.pallas_call(
        functools.partial(image_kernel, count),
        out_shape=pltpu.VMEM((2, TILE_X, bins), jnp.bfloat16),
        in_specs=[pl.BlockSpec(memory_space=pltpu.HBM)] * 7,
        out_specs=pl.BlockSpec(memory_space=pltpu.VMEM),
        scratch_shapes=[
            pltpu.SMEM(tile_anchor.shape, jnp.int32),
            pltpu.SMEM(integer_cell_displacement.shape, jnp.int32),
            pltpu.SMEM(fractional_level_label.shape, jnp.int32),
            pltpu.SMEM(scalars.shape, jnp.float32),
            pltpu.VMEM(echoes.shape, echoes.dtype),
            pltpu.VMEM(steering.shape, steering.dtype),
            pltpu.VMEM(table.shape, table.dtype),
            dma((6 + pulses,)),
            pltpu.VMEM((pulses, HALVES, channels, 2 * LANES), jnp.bfloat16),
            pltpu.VMEM((2, beams, channels), jnp.bfloat16),
            pltpu.VMEM((CHUNKS, pulses, beams, LANES), jnp.bfloat16),
            pltpu.VMEM((CHUNKS, GROUP, pulses, beams, LANES), jnp.bfloat16),
            pltpu.VMEM((GROUP, pulses, beams, LANES), jnp.bfloat16),
            pltpu.VMEM((REACH - 1, PAIR, CHUNKS, *narrow), jnp.float32),
            pltpu.VMEM((CHUNKS, *narrow), jnp.float32),
            pltpu.VMEM((HALVES, CHUNKS, *narrow), jnp.float32),
            pltpu.VMEM((REACH, PAIR, CHUNKS, *narrow), jnp.bfloat16),
            pltpu.VMEM((REACH - 1, PAIR, CHUNKS, *narrow), jnp.bfloat16),
            pltpu.VMEM((HALVES, CHUNKS, *narrow), jnp.bfloat16),
            pltpu.VMEM((CHUNKS, *narrow), jnp.bfloat16),
            pltpu.VMEM((CHUNKS, *narrow), jnp.bfloat16),
            dma((2, pulses)), dma((2, pulses)), dma((2, pulses)), dma((2, pulses)),
            dma(pair), dma(pair), dma(pair), dma(pair), dma(pair), dma(pair),
            dma((REACH - 1, PAIR, CHUNKS)), dma((REACH - 1, PAIR, CHUNKS)),
            dma((PAIR, CHUNKS)), dma((HALVES, CHUNKS)), dma((CHUNKS,)), dma((CHUNKS,)),
        ],
        compiler_params=pltpu.CompilerParams(
            collective_id=0, has_side_effects=True, vmem_limit_bytes=66_781_184
        ),
        name="image",
    )(tile_anchor, integer_cell_displacement, fractional_level_label, scalars, echoes, steering, table)


def solution(mesh):
    placed = (
        P(None, ("scene", "along"), None, None, None),
        P(("scene", "along"), None),
        P(("scene", "along"), None),
        P(),
        P("scene"),
    )
    return jax.shard_map(
        functools.partial(local, mesh.shape["along"]),
        mesh=mesh,
        in_specs=placed,
        out_specs=P(None, ("scene", "along"), None),
        check_vma=False,
    )
```
